32 devices in a mesh: seq: 8 (over z, y), chan: 4 (over x, core).
Axes of the slice: x: 2, y: 2, z: 4, core: 2. Of those that a mesh axis runs over, the one named last changes fastest.
Arguments:
- inputs: bfloat16 [4096, 4096], P('seq', 'chan'), may hold values from -6 to 6
- out_grad: bfloat16 [4096, 4096], P('seq', 'chan'), may hold values from -0.0048828125 to 0.0048828125
- embed_weight: float32 [17, 64], replicated, may hold values from -1.5 to 1.5
- embed_bias: float32 [64], replicated, may hold values from -1 to 1
- embed_freq: float32 [64], replicated, may hold values from 0.5 to 2
- mixer_weight: float32 [64, 64], replicated, may hold values from -0.75 to 0.75
- mixer_bias: float32 [64], replicated, may hold values from -1 to 1
- mixer_freq: float32 [64], replicated, may hold values from 0.5 to 2
- head_weight: float32 [64, 4096], P(None, 'chan'), may hold values from -0.75 to 0.75
- decay_rates: float32 [4096], P('chan'), may hold values from 1 to 12
Outputs:
- embed_weight_grad: float32 [17, 64], replicated
- embed_bias_grad: float32 [64], replicated
- embed_freq_grad: float32 [64], replicated
- mixer_weight_grad: float32 [64, 64], replicated
- mixer_bias_grad: float32 [64], replicated
- mixer_freq_grad: float32 [64], replicated
- head_weight_grad: float32 [64, 4096], P(None, 'chan')
- decay_rates_grad: float32 [4096], P('chan')
The draws below stay inside these ranges and needn't reach their ends.
All inputs are finite; a program needn't handle non-finite values.
Results may differ from the reference program's by a relative error of at most 0.0003.
Values may be sent and summed in bfloat16 or wider, within the bound.
No kernel may reach another device: no remote copies, remote signals or barrier semaphores. Data moves between devices by JAX's collectives and lax.ppermute only.
A program may use at most 128 MiB of HBM per device.

```python
import math
import jax
import jax.numpy as jnp
from jax import lax

CHANNELS = 4096
NET_HIDDEN = 64
BANDS = 8
FEATURES = 17
FILTER_LEN = 1536
TOKENS = 4096


def levels(rng, dims, shards, least, top_value):
    def one(dim, shards_of):
        steps = jax.random.uniform(jax.random.fold_in(jax.random.fold_in(rng, 6), dim), (shards_of,), jnp.float32, least / len(shards), top_value / len(shards))
        return jnp.repeat(jnp.exp(steps), dims[dim] // shards_of).reshape((-1,) + (1,) * (len(dims) - dim - 1))

    factor_of = one(*shards[0])
    for cut in shards[1:]:
        factor_of = factor_of * one(*cut)
    return factor_of


def noise(own_key, shape, width, most, shards=(), kind=jnp.bfloat16):
    result = width * jax.random.normal(own_key, shape, jnp.float32)
    if shards:
        result = result * levels(own_key, shape, shards, -0.22, 0.18)
    return jnp.clip(result, -most, most).astype(kind)


def setup_inputs(seed: int = 0) -> dict:
    seeds = jax.random.split(jax.random.key(seed), 11)
    inputs = noise(seeds[0], (TOKENS, CHANNELS), 1.0, 6.0, ((0, 8), (1, 4)))
    out_grad = noise(seeds[1], (TOKENS, CHANNELS), (2.0 / (TOKENS * FILTER_LEN) ** 0.5), 0.0048828125, ((0, 8), (1, 4)))
    embed_weight = noise(seeds[2], (FEATURES, NET_HIDDEN), FEATURES ** -0.5, 1.5, (), jnp.float32)
    embed_bias = jnp.clip(jax.random.uniform(seeds[3], (NET_HIDDEN,), jnp.float32, -1.0, 1.0), -1.0, 1.0)
    embed_freq = jnp.clip(jnp.exp(jax.random.uniform(seeds[4], (NET_HIDDEN,), jnp.float32, math.log(0.5), math.log(2.0))), 0.5, 2.0)
    mixer_weight = noise(seeds[5], (NET_HIDDEN, NET_HIDDEN), NET_HIDDEN ** -0.5, 0.75, (), jnp.float32)
    mixer_bias = jnp.clip(jax.random.uniform(seeds[6], (NET_HIDDEN,), jnp.float32, -1.0, 1.0), -1.0, 1.0)
    mixer_freq = jnp.clip(jnp.exp(jax.random.uniform(seeds[7], (NET_HIDDEN,), jnp.float32, math.log(0.5), math.log(2.0))), 0.5, 2.0)
    head_weight = noise(seeds[8], (NET_HIDDEN, CHANNELS), NET_HIDDEN ** -0.5, 0.75, ((1, 4),), jnp.float32)
    decay_rates = jnp.clip(jnp.exp(math.log(12.0) - 2.4849066 * jax.random.uniform(seeds[9], (CHANNELS,), jnp.float32) ** levels(seeds[9], (CHANNELS,), ((0, 4),), -0.2, 0.2)), 1.0, 12.0)
    return {"inputs": inputs, "out_grad": out_grad, "embed_weight": embed_weight, "embed_bias": embed_bias, "embed_freq": embed_freq, "mixer_weight": mixer_weight, "mixer_bias": mixer_bias, "mixer_freq": mixer_freq, "head_weight": head_weight, "decay_rates": decay_rates}


EXACT = lax.Precision.HIGHEST

def tap_features(tap_index, filter_len, band_count):
    scaled = tap_index.astype(jnp.float32) / filter_len
    band_freqs = jnp.array([max(1, filter_len // 4 // 2 ** (band_count - band_level)) for band_level in range(1, band_count + 1)], dtype=jnp.int32)
    cycles = band_freqs[:, None] * tap_index[None, :] % filter_len
    band_angle = cycles.astype(jnp.float32) * (2.0 * math.pi / filter_len)
    return (scaled, jnp.concatenate([scaled[None, :], jnp.cos(band_angle), jnp.sin(band_angle)], axis=0))

def filter_values(embed_weight, embed_bias, embed_freq, mixer_weight, mixer_bias, mixer_freq, head_weight, decay_rates):
    tap_index = jnp.arange(FILTER_LEN, dtype=jnp.int32)
    scaled, features = tap_features(tap_index, FILTER_LEN, BANDS)
    first_pre = jnp.dot(embed_weight.T, features, precision=EXACT, preferred_element_type=jnp.float32) + embed_bias[:, None]
    first_act = jnp.sin(embed_freq[:, None] * first_pre)
    second_pre = jnp.dot(mixer_weight.T, first_act, precision=EXACT, preferred_element_type=jnp.float32) + mixer_bias[:, None]
    second_act = jnp.sin(mixer_freq[:, None] * second_pre)
    shaped = jnp.dot(second_act.T, head_weight, precision=EXACT, preferred_element_type=jnp.float32)
    return shaped * jnp.exp(-scaled[:, None] * decay_rates[None, :])

def correlate_group(pair):
    group_in, group_grad = pair
    fft_length = 2 * TOKENS
    in_spec = jnp.fft.rfft(group_in, n=fft_length, axis=0)
    grad_spec = jnp.fft.rfft(group_grad, n=fft_length, axis=0)
    return jnp.fft.irfft(jnp.conj(in_spec) * grad_spec, n=fft_length, axis=0)[:FILTER_LEN]

def reference(inputs, out_grad, embed_weight, embed_bias, embed_freq, mixer_weight, mixer_bias, mixer_freq, head_weight, decay_rates):
    group_size = 128
    group_count = CHANNELS // group_size
    in_groups = inputs.astype(jnp.float32).reshape(TOKENS, group_count, group_size).transpose(1, 0, 2)
    grad_groups = out_grad.astype(jnp.float32).reshape(TOKENS, group_count, group_size).transpose(1, 0, 2)
    filter_grad = lax.map(correlate_group, (in_groups, grad_groups))
    filter_grad = filter_grad.transpose(1, 0, 2).reshape(FILTER_LEN, CHANNELS)
    filter_now, pullback = jax.vjp(filter_values, embed_weight, embed_bias, embed_freq, mixer_weight, mixer_bias, mixer_freq, head_weight, decay_rates)
    grad_ew, grad_eb, grad_ef, grad_mw, grad_mb, grad_mf, grad_hw, grad_dr = pullback(filter_grad)
    return (grad_ew, grad_eb, grad_ef, grad_mw, grad_mb, grad_mf, grad_hw, grad_dr)
```

```python
import functools
import math

import jax
import jax.numpy as jnp
import numpy as np
from jax import lax
from jax.experimental import pallas as pl
from jax.experimental.pallas import tpu as pltpu
from jax.sharding import PartitionSpec as P

BANDS = 8
SPAN_PARTS = 3
EXACT = lax.Precision.HIGHEST


def shifted(value, axis, steps):
    count = lax.axis_size(axis)
    first, last = (max(0, -steps), min(count, count - steps))
    return lax.ppermute(value, axis, [(source, source + steps) for source in range(first, last)])


def swapped(value, axis, bit):
    return lax.ppermute(value, axis, [(i, i ^ bit) for i in range(lax.axis_size(axis))])


def bits_of(axis, first=1):
    count = lax.axis_size(axis)
    assert count & (count - 1) == 0
    return [1 << i for i in range(count.bit_length() - 1) if (1 << i) >= first]


def split_const(matrix):
    high = matrix.astype(np.float32).astype(jnp.bfloat16)
    low = (matrix - high.astype(np.float64)).astype(np.float32).astype(jnp.bfloat16)
    return high, low


@functools.cache
def transforms(size):
    freqs = np.concatenate([np.arange(0, size, 2), np.arange(1, size, 2)])
    omega = np.pi * (2 * freqs + 1) / (2 * size)
    steps = np.arange(size)
    forward = np.concatenate(
        [np.cos(omega[:, None] * steps), -np.sin(omega[:, None] * steps)], axis=0
    )
    dist = size - steps
    inverse = (
        np.concatenate(
            [np.cos(dist[:, None] * omega), -np.sin(dist[:, None] * omega)], axis=1
        )
        / size
    )
    return split_const(forward), split_const(inverse)


def split_pair(value):
    high = value.astype(jnp.bfloat16)
    return high, (value - high.astype(jnp.float32)).astype(jnp.bfloat16)


def split_outer(value):
    high = lax.reduce_precision(value, 8, 7)
    return high.astype(jnp.bfloat16), (value - high).astype(jnp.bfloat16)


def tap_features(tap_index, filter_len, band_count):
    scaled = tap_index.astype(jnp.float32) / filter_len
    band_freqs = jnp.array(
        [
            max(1, filter_len // 4 // 2 ** (band_count - band_level))
            for band_level in range(1, band_count + 1)
        ],
        dtype=jnp.int32,
    )
    cycles = band_freqs[:, None] * tap_index[None, :] % filter_len
    band_angle = cycles.astype(jnp.float32) * (2.0 * math.pi / filter_len)
    return (
        scaled,
        jnp.concatenate([scaled[None, :], jnp.cos(band_angle), jnp.sin(band_angle)], axis=0),
    )


def dot32(left, right, dims=(((1,), (0,)), ((), ()))):
    return lax.dot_general(
        left, right, dims, precision=EXACT, preferred_element_type=jnp.float32
    )


def dot16(left, right, dims=(((1,), (0,)), ((), ()))):
    return lax.dot_general(left, right, dims, preferred_element_type=jnp.float32)


NT = (((1,), (1,)), ((), ()))


def own_pairs():
    return [(b, j, b - j) for j in range(4) for b in range(j, 4)]


def cross_pairs(groups):
    return [(b, j, b + 4 - j) for j in range(5) for b in range(4) if b + 4 - j < groups]


def main_kernel(
    size,
    groups,
    filter_len,
    par_ref,
    xk_ref,
    gk_ref,
    e1_ref,
    e2_ref,
    xp_ref,
    gn_ref,
    s3_ref,
    fwd_ref,
    inv_ref,
    invlo_ref,
    acth_ref,
    actl_ref,
    headh_ref,
    headl_ref,
    head_ref,
    rates_ref,
    part_ref,
    second_ref,
    spec,
    prod,
):
    step = pl.program_id(0)
    par = par_ref[0]
    width = xk_ref.shape[1]
    hidden = head_ref.shape[0]

    def transform(ref, slot):
        for i in range(2):
            block = ref[i * size : (i + 1) * size, :]
            spec[slot + i] = dot16(fwd_ref[...], jnp.concatenate([block, block], axis=0))

    transform(xk_ref, 4 + 2 * par)
    transform(gk_ref, 8 + 2 * par)
    transform(xp_ref, 2 * par)
    transform(gn_ref, 12 + 2 * par)
    transform(e1_ref, 6 + 2 * par)
    transform(e2_ref, 10 - 6 * par)
    transform(s3_ref, 2 + 10 * par)

    lanes = 128
    rows = 16
    per_half = size // 2 // rows

    def products(sign, base):
        def body(it, carry):
            row = pl.multiple_of(base + (it % per_half) * rows, rows)
            lane = pl.multiple_of((it // per_half) * lanes, lanes)

            def load(slot):
                return (
                    spec[slot, pl.ds(row, rows), pl.ds(lane, lanes)],
                    spec[slot, pl.ds(row + size, rows), pl.ds(lane, lanes)],
                )

            acc_re = [None] * groups
            acc_im = [None] * groups

            def add(m, g, w):
                re = g[0] * w[0] + g[1] * w[1]
                im = g[0] * w[1] - g[1] * w[0]
                acc_re[m] = re if acc_re[m] is None else acc_re[m] + re
                acc_im[m] = im if acc_im[m] is None else acc_im[m] + im

            def turned(v):
                return (v[1], -v[0]) if sign > 0 else (-v[1], v[0])

            def window(early, late):
                if late is None:
                    return early
                if early is None:
                    return turned(late)
                if sign > 0:
                    return (early[0] + late[1], early[1] - late[0])
                return (early[0] - late[1], early[1] + late[0])

            def run(xbase, gbase, count, gcount, pairs):
                gs = [load(gbase + b) for b in range(gcount)]
                prev = None
                for j in range(count + 1):
                    now = load(xbase + j) if j < count else None
                    todo = [(b, m) for b, jj, m in pairs if jj == j]
                    if todo:
                        w = window(prev, now)
                        for b, m in todo:
                            add(m, gs[b], w)
                    prev = now

            run(4, 8, 4, 4, own_pairs())
            run(4 * par, 8 + 4 * par, 4, 4, cross_pairs(groups))
            run(2, 12, 2, 2, [(0, 1, 5), (0, 2, 4), (1, 2, 5)])
            for m in range(groups):
                for part, value in enumerate((acc_re[m], acc_im[m])):
                    high, low = split_pair(value)
                    prod[m, pl.ds(row + part * size, rows), pl.ds(lane, lanes)] = high
                    prod[m, pl.ds(row + (2 + part) * size, rows), pl.ds(lane, lanes)] = low
            return carry

        lax.fori_loop(0, per_half * (width // lanes), body, 0)

    products(1, 0)
    products(-1, size // 2)

    total = jnp.zeros((2 * hidden, width), jnp.float32)
    for m in range(groups):
        grad = dot16(inv_ref[...], prod[m]) + dot16(invlo_ref[...], prod[m, : 2 * size, :])
        tap = lax.broadcasted_iota(jnp.int32, (size, width), 0) + m * size
        place = tap.astype(jnp.float32) / filter_len
        delta = grad * jnp.exp(-place * rates_ref[...])
        high, low = split_pair(delta)
        cols = slice(m * size, (m + 1) * size)
        total += (
            dot16(acth_ref[:, cols], high)
            + dot16(acth_ref[:, cols], low)
            + dot16(actl_ref[:, cols], high)
        )
        second = (
            dot16(headh_ref[...], high, NT)
            + dot16(headh_ref[...], low, NT)
            + dot16(headl_ref[...], high, NT)
        )

        @pl.when(step == 0)
        def _():
            second_ref[:, cols] = second

        @pl.when(step > 0)
        def _():
            second_ref[:, cols] += second

    part_ref[:hidden, :] = total[:hidden]
    part_ref[hidden:, :] = jnp.broadcast_to(
        -jnp.sum(total[hidden:] * head_ref[...], axis=0, keepdims=True),
        (part_ref.shape[0] - hidden, width),
    )


def shards(
    inputs,
    out_grad,
    embed_weight,
    embed_bias,
    embed_freq,
    mixer_weight,
    mixer_bias,
    mixer_freq,
    head_weight,
    decay_rates,
):
    block_len, chan_count = inputs.shape
    hidden = head_weight.shape[0]
    half = chan_count // 2
    size = block_len // 2
    filter_len = SPAN_PARTS * block_len
    groups = filter_len // size
    seq_index = lax.axis_index("seq")
    par = seq_index % 2

    def part_of(value, which):
        return lax.dynamic_slice_in_dim(value, which * half, half, axis=1)

    x_keep = part_of(inputs, par)
    g_keep = part_of(out_grad, par)
    x_give = part_of(inputs, 1 - par)
    g_give = part_of(out_grad, 1 - par)
    first = jnp.where(par == 0, g_give, x_give)
    other = jnp.where(par == 0, x_give, g_give)
    e1 = swapped(first, "seq", 1)
    x_prev = shifted(x_keep, "seq", 2)
    g_next = shifted(g_keep, "seq", -2)
    e1, other = lax.optimization_barrier((e1, other))
    e2 = swapped(other, "seq", 1)
    count = lax.axis_size("seq")
    s3 = lax.ppermute(
        e1,
        "seq",
        [(i, i + 2) for i in range(0, count - 2, 2)] + [(i, i - 2) for i in range(3, count, 2)],
    )

    scaled, features = tap_features(jnp.arange(filter_len, dtype=jnp.int32), filter_len, BANDS)
    first_pre = dot32(embed_weight.T, features) + embed_bias[:, None]
    first_act = jnp.sin(embed_freq[:, None] * first_pre)
    second_pre = dot32(mixer_weight.T, first_act) + mixer_bias[:, None]
    second_act = jnp.sin(mixer_freq[:, None] * second_pre)
    act_high, act_low = split_outer(
        jnp.concatenate([second_act, second_act * scaled[None, :]], axis=0)
    )
    head_own = part_of(head_weight, par)
    head_high, head_low = split_outer(head_own)
    rates_own = lax.dynamic_slice_in_dim(decay_rates, par * half, half)[None, :]

    (fwd_high, fwd_low), (inv_high, inv_low) = transforms(size)
    forward = np.concatenate([fwd_high, fwd_low], axis=1)
    inverse = np.concatenate([inv_high, inv_high], axis=1)

    width = min(256, half)

    def whole(shape):
        return pl.BlockSpec(shape, lambda i: (0,) * len(shape))

    def tiled(rows):
        return pl.BlockSpec((rows, width), lambda i: (0, i))

    part, second_grad = pl.pallas_call(
        functools.partial(main_kernel, size, groups, filter_len),
        grid=(half // width,),
        in_specs=[pl.BlockSpec(memory_space=pltpu.SMEM)]
        + [tiled(block_len)] * 7
        + [
            whole((2 * size, 2 * size)),
            whole((size, 4 * size)),
            whole((size, 2 * size)),
            whole((2 * hidden, filter_len)),
            whole((2 * hidden, filter_len)),
            tiled(hidden),
            tiled(hidden),
            tiled(hidden),
            tiled(1),
        ],
        out_specs=[tiled(hidden + 8), whole((hidden, filter_len))],
        out_shape=[
            jax.ShapeDtypeStruct((hidden + 8, half), jnp.float32),
            jax.ShapeDtypeStruct((hidden, filter_len), jnp.float32),
        ],
        scratch_shapes=[
            pltpu.VMEM((16, 2 * size, width), jnp.float32),
            pltpu.VMEM((groups, 4 * size, width), jnp.bfloat16),
        ],
        compiler_params=pltpu.CompilerParams(vmem_limit_bytes=60 * 2**20),
        name="filter_grad",
    )(
        par.reshape(1),
        x_keep,
        g_keep,
        e1,
        e2,
        x_prev,
        g_next,
        s3,
        jnp.asarray(forward),
        jnp.asarray(inverse),
        jnp.asarray(inv_low),
        act_high,
        act_low,
        head_high,
        head_low,
        head_own,
        rates_own,
    )

    for bit in bits_of("seq", 2):
        part = part + swapped(part, "seq", bit)
    mate = swapped(part, "seq", 1)
    full = jnp.where(
        par == 0,
        jnp.concatenate([part, mate], axis=1),
        jnp.concatenate([mate, part], axis=1),
    )
    grad_head = full[:hidden]
    grad_rates = full[hidden]

    second_slope = jnp.cos(mixer_freq[:, None] * second_pre) * second_grad
    second_delta = second_slope * mixer_freq[:, None]
    first_grad = dot32(mixer_weight, second_delta)
    first_slope = jnp.cos(embed_freq[:, None] * first_pre) * first_grad
    first_delta = first_slope * embed_freq[:, None]
    net = jnp.concatenate(
        [
            dot32(second_delta, first_act, NT),
            dot32(first_delta, features, NT),
            jnp.sum(first_delta, axis=1, keepdims=True),
            jnp.sum(first_slope * first_pre, axis=1, keepdims=True),
            jnp.sum(second_delta, axis=1, keepdims=True),
            jnp.sum(second_slope * second_pre, axis=1, keepdims=True),
        ],
        axis=1,
    )
    for axis in ("chan", "seq"):
        for bit in bits_of(axis):
            net = net + swapped(net, axis, bit)
    rows = net.shape[0]
    feats = features.shape[0]
    return (
        net[:, rows : rows + feats].T,
        net[:, rows + feats],
        net[:, rows + feats + 1],
        net[:, :rows].T,
        net[:, rows + feats + 2],
        net[:, rows + feats + 3],
        grad_head,
        grad_rates,
    )


def solution(mesh):
    in_specs = (
        P("seq", "chan"),
        P("seq", "chan"),
        P(),
        P(),
        P(),
        P(),
        P(),
        P(),
        P(None, "chan"),
        P("chan"),
    )
    out_specs = (P(), P(), P(), P(), P(), P(), P(None, "chan"), P("chan"))
    return jax.shard_map(shards, mesh=mesh, in_specs=in_specs, out_specs=out_specs, check_vma=False)
```

```python
import functools
import math

import jax
import jax.numpy as jnp
import numpy as np
from jax import lax
from jax.experimental import pallas as pl
from jax.experimental.pallas import tpu as pltpu
from jax.sharding import PartitionSpec as P

BANDS = 8
SPAN_PARTS = 3
EXACT = lax.Precision.HIGHEST


def shifted(value, axis, steps):
    count = lax.axis_size(axis)
    first, last = (max(0, -steps), min(count, count - steps))
    return lax.ppermute(value, axis, [(source, source + steps) for source in range(first, last)])


def swapped(value, axis, bit):
    return lax.ppermute(value, axis, [(i, i ^ bit) for i in range(lax.axis_size(axis))])


def bits_of(axis, first=1):
    count = lax.axis_size(axis)
    assert count & (count - 1) == 0
    return [1 << i for i in range(count.bit_length() - 1) if (1 << i) >= first]


def split_const(matrix):
    high = matrix.astype(np.float32).astype(jnp.bfloat16)
    low = (matrix - high.astype(np.float64)).astype(np.float32).astype(jnp.bfloat16)
    return high, low


@functools.cache
def transforms(size):
    freqs = np.arange(0, size, 2)
    freqs = np.concatenate([freqs, size - 1 - freqs])
    omega = np.pi * (2 * freqs + 1) / (2 * size)
    steps = np.arange(size)
    forward = np.concatenate(
        [np.cos(omega[:, None] * steps), -np.sin(omega[:, None] * steps)], axis=0
    )
    omega = omega[: size // 2]
    dist = size - tap_order(size)
    inverse = (
        np.concatenate(
            [np.cos(dist[:, None] * omega), -np.sin(dist[:, None] * omega)], axis=1
        )
        / size
    )
    return split_const(forward), split_const(inverse)


def tap_order(size):
    return np.concatenate([np.arange(0, size, 2), np.arange(1, size, 2)])


def split_pair(value):
    high = value.astype(jnp.bfloat16)
    return high, (value - high.astype(jnp.float32)).astype(jnp.bfloat16)


def split_outer(value):
    high = lax.reduce_precision(value, 8, 7)
    return high.astype(jnp.bfloat16), (value - high).astype(jnp.bfloat16)


def tap_features(tap_index, filter_len, band_count):
    scaled = tap_index.astype(jnp.float32) / filter_len
    band_freqs = jnp.array(
        [
            max(1, filter_len // 4 // 2 ** (band_count - band_level))
            for band_level in range(1, band_count + 1)
        ],
        dtype=jnp.int32,
    )
    cycles = band_freqs[:, None] * tap_index[None, :] % filter_len
    band_angle = cycles.astype(jnp.float32) * (2.0 * math.pi / filter_len)
    return (
        scaled,
        jnp.concatenate([scaled[None, :], jnp.cos(band_angle), jnp.sin(band_angle)], axis=0),
    )


def dot32(left, right, dims=(((1,), (0,)), ((), ()))):
    return lax.dot_general(
        left, right, dims, precision=EXACT, preferred_element_type=jnp.float32
    )


def dot16(left, right, dims=(((1,), (0,)), ((), ()))):
    return lax.dot_general(left, right, dims, preferred_element_type=jnp.float32)


NT = (((1,), (1,)), ((), ()))
FIXED, BEYOND, WINDOWED = 0, 4, 6


def block_pairs(groups):
    return [(b, j, b + 4 - j) for j in range(8) for b in range(4) if 0 <= b + 4 - j < groups]


def main_kernel(
    size,
    groups,
    filter_len,
    first,
    last,
    par_ref,
    xk_ref,
    gk_ref,
    e1_ref,
    e2_ref,
    xp_ref,
    gn_ref,
    s3_ref,
    fwd_ref,
    inv_ref,
    acth_ref,
    actl_ref,
    head_ref,
    rates_ref,
    *rest,
):
    rest = list(rest)
    second_in = None if first else rest.pop(0)
    if last:
        net_in, rest = rest[:9], rest[9:]
        part_ref, net_ref, spec, prod, hold, second_ref = rest
    else:
        part_ref, second_ref, spec, prod, hold = rest
    par = par_ref[0]
    width = xk_ref.shape[1]
    hidden = head_ref.shape[0]
    mid = size // 2

    def transform(ref, slot):
        for i in range(2):
            block = ref[i * size : (i + 1) * size, :]
            spec[slot + (i ^ par)] = dot16(fwd_ref[...], jnp.concatenate([block, block], axis=0))

    transform(xk_ref, (WINDOWED + 4) * (1 - par))
    transform(gk_ref, (WINDOWED + 4) * par)
    transform(xp_ref, WINDOWED - 2 * par)
    transform(gn_ref, BEYOND + 2 * par)
    transform(e1_ref, WINDOWED + 6)
    transform(e2_ref, FIXED + 2)
    transform(s3_ref, WINDOWED + 2)

    lanes = 128
    rows = 16
    tiles = mid // rows

    def products(row, lane, sign):
        def load(slot):
            return (
                spec[slot, pl.ds(row, rows), pl.ds(lane, lanes)],
                spec[slot, pl.ds(row + size, rows), pl.ds(lane, lanes)],
            )

        acc_re = [None] * groups
        acc_im = [None] * groups

        def add(m, g, w):
            re = g[0] * w[0] + g[1] * w[1]
            im = g[0] * w[1] - g[1] * w[0]
            acc_re[m] = re if acc_re[m] is None else acc_re[m] + re
            acc_im[m] = im if acc_im[m] is None else acc_im[m] + im

        fixed = [load(FIXED + b) for b in range(4)]
        prev = None
        for j in range(8):
            now = load(WINDOWED + j)
            if prev is None:
                w = (now[1], -now[0]) if sign > 0 else (-now[1], now[0])
            elif sign > 0:
                w = (prev[0] + now[1], prev[1] - now[0])
            else:
                w = (prev[0] - now[1], prev[1] + now[0])
            for b, jj, m in block_pairs(groups):
                if jj == j:
                    add(m, fixed[b], w)
            if j == 3:
                near, far = load(BEYOND), load(BEYOND + 1)
                add(5, near, w)
                add(4, near, now)
                add(5, far, now)
            prev = now
        return acc_re, acc_im

    def body(it, carry):
        row = pl.multiple_of((it % tiles) * rows, rows)
        lane = pl.multiple_of((it // tiles) * lanes, lanes)
        even_re, even_im = products(row, lane, 1)
        for m in range(groups):
            hold[2 * m] = even_re[m]
            hold[2 * m + 1] = even_im[m]
        odd_re, odd_im = products(row + mid, lane, -1)
        for m in range(groups):
            re, im = hold[2 * m], hold[2 * m + 1]
            folded = (re + odd_re[m], im - odd_im[m], re - odd_re[m], im + odd_im[m])
            for part, value in enumerate(folded):
                high, low = split_pair(value)
                at = (pl.ds(row + part * mid, rows), pl.ds(lane, lanes))
                prod[2 * m, at[0], at[1]] = high
                prod[2 * m + 1, at[0], at[1]] = low
        return carry

    lax.fori_loop(0, tiles * (width // lanes), body, 0)

    rates = rates_ref[...]
    tap = lax.broadcasted_iota(jnp.int32, (size, width), 0)
    tap = jnp.where(tap < mid, 2 * tap, 2 * (tap - mid) + 1)
    inner = jnp.exp(-(tap.astype(jnp.float32) / filter_len) * rates)
    head_high, head_low = split_pair(head_ref[...])
    total = jnp.zeros((2 * hidden, width), jnp.float32)
    for m in range(groups):
        grads = []
        for q in range(2):
            high = prod[2 * m, q * size : (q + 1) * size, :]
            low = prod[2 * m + 1, q * size : (q + 1) * size, :]
            both = dot16(inv_ref[q], high)
            grads.append(both[:mid] + both[mid:] + dot16(inv_ref[q, :mid, :], low))
        outer = jnp.exp(-(m * size / filter_len) * rates)
        delta = jnp.concatenate(grads, axis=0) * (inner * outer)
        high, low = split_pair(delta)
        cols = slice(m * size, (m + 1) * size)
        total += (
            dot16(acth_ref[:, cols], high)
            + dot16(acth_ref[:, cols], low)
            + dot16(actl_ref[:, cols], high)
        )
        second = (
            dot16(head_high, high, NT) + dot16(head_high, low, NT) + dot16(head_low, high, NT)
        )
        second_ref[:, cols] = second if first else second + second_in[:, cols]

    part_ref[:hidden, :] = total[:hidden]
    part_ref[hidden:, :] = jnp.broadcast_to(
        -jnp.sum(total[hidden:] * head_ref[...], axis=0, keepdims=True),
        (part_ref.shape[0] - hidden, width),
    )

    if last:
        mix, mix_freq, emb_freq, feats, pre1, act1, cos1, pre2, cos2 = (r[...] for r in net_in)
        slope2 = second_ref[...] * cos2
        delta2 = slope2 * mix_freq
        slope1 = dot32(mix, delta2) * cos1
        delta1 = slope1 * emb_freq
        count = feats.shape[0]
        net_ref[:, :hidden] = dot32(delta2, act1, NT)
        net_ref[:, hidden : hidden + count] = dot32(delta1, feats, NT)
        for i, value in enumerate((delta1, slope1 * pre1, delta2, slope2 * pre2)):
            at = hidden + count + i
            net_ref[:, at : at + 1] = jnp.sum(value, axis=1, keepdims=True)
        at = hidden + count + 4
        net_ref[:, at:] = jnp.zeros((hidden, net_ref.shape[1] - at), jnp.float32)


def finish_kernel(count, par_ref, net_ref, far_ref, *rest):
    ew_ref, eb_ref, ef_ref, mw_ref, mb_ref, mf_ref, head_ref, rates_ref = rest[-8:]
    parts = rest[:-8]
    par = par_ref[0]
    turned = (net_ref[...] + far_ref[...]).T
    hidden = turned.shape[1]
    mw_ref[...] = turned[:hidden]
    ew_ref[...] = turned[hidden : hidden + count]
    for i, ref in enumerate((eb_ref, ef_ref, mb_ref, mf_ref)):
        ref[...] = turned[hidden + count + i : hidden + count + i + 1]
    width = parts[0].shape[1]
    half = head_ref.shape[1] // 2
    for i in range(len(parts) // 2):
        for which, ref in ((par, parts[2 * i]), (1 - par, parts[2 * i + 1])):
            at = pl.ds(pl.multiple_of(which * half + i * width, width), width)
            head_ref[:, at] = ref[:hidden, :]
            rates_ref[:, at] = ref[hidden : hidden + 1, :]


def after(value, *others):
    return lax.optimization_barrier((value, *others))[0]


def shards(
    inputs,
    out_grad,
    embed_weight,
    embed_bias,
    embed_freq,
    mixer_weight,
    mixer_bias,
    mixer_freq,
    head_weight,
    decay_rates,
):
    block_len, chan_count = inputs.shape
    hidden = head_weight.shape[0]
    half = chan_count // 2
    size = block_len // 2
    filter_len = SPAN_PARTS * block_len
    groups = filter_len // size
    par = lax.axis_index("seq") % 2
    count = lax.axis_size("seq")
    width = min(256, half)
    chunks = range(half // width)

    def part_of(value, which, chunk, span):
        start = which * half + chunk * span
        return lax.dynamic_slice_in_dim(value, start, span, axis=1)

    def gives(chunk):
        x_give = part_of(inputs, 1 - par, chunk, width)
        g_give = part_of(out_grad, 1 - par, chunk, width)
        return jnp.where(par == 0, g_give, x_give), jnp.where(par == 0, x_give, g_give)

    x_keep = part_of(inputs, par, 0, half)
    g_keep = part_of(out_grad, par, 0, half)
    ahead = [(i, i + 2) for i in range(0, count - 2, 2)]
    back = [(i, i - 2) for i in range(3, count, 2)]
    e1, e2, s3 = [], [], []
    x_prev = g_next = None
    last_in = None
    for c in chunks:
        one, two = gives(c)
        if last_in is not None:
            one = after(one, last_in)
        got = swapped(one, "seq", 1)
        if x_prev is None:
            x_prev = shifted(x_keep, "seq", 2)
            g_next = shifted(g_keep, "seq", -2)
        two, got = lax.optimization_barrier((two, got))
        e1.append(got)
        e2.append(swapped(two, "seq", 1))
        s3.append(lax.ppermute(got, "seq", ahead + back))
        last_in = e2[-1]

    order = np.concatenate([m * size + tap_order(size) for m in range(groups)])
    scaled, features = tap_features(jnp.asarray(order.astype(np.int32)), filter_len, BANDS)
    first_pre = dot32(embed_weight.T, features) + embed_bias[:, None]
    first_act = jnp.sin(embed_freq[:, None] * first_pre)
    first_cos = jnp.cos(embed_freq[:, None] * first_pre)
    second_pre = dot32(mixer_weight.T, first_act) + mixer_bias[:, None]
    second_act = jnp.sin(mixer_freq[:, None] * second_pre)
    second_cos = jnp.cos(mixer_freq[:, None] * second_pre)
    act_high, act_low = split_outer(
        jnp.concatenate([second_act, second_act * scaled[None, :]], axis=0)
    )

    (fwd_high, fwd_low), (inv_high, inv_low) = transforms(size)
    forward = np.concatenate([fwd_high, fwd_low], axis=1)
    turn = jnp.where(
        (par == 1) & (jnp.arange(2 * size) >= size), -1.0, 1.0
    ).astype(jnp.bfloat16)
    forward = jnp.asarray(forward) * turn[:, None]
    mid = size // 2
    inverse = jnp.asarray(
        np.stack(
            [
                np.concatenate([inv_high[q * mid : (q + 1) * mid], inv_low[q * mid : (q + 1) * mid]])
                for q in range(2)
            ]
        )
    )

    parts = []
    second_grad = None
    for c in chunks:
        first, last = c == 0, c == chunks[-1]
        here = slice(c * width, (c + 1) * width)
        operands = [
            par.reshape(1),
            x_keep[:, here],
            g_keep[:, here],
            e1[c],
            e2[c],
            x_prev[:, here],
            g_next[:, here],
            s3[c],
            forward,
            inverse,
            act_high,
            act_low,
            part_of(head_weight, par, c, width),
            lax.dynamic_slice_in_dim(decay_rates, par * half + c * width, width)[None, :],
        ]
        if not first:
            operands.append(second_grad)
        part_shape = jax.ShapeDtypeStruct((hidden + 8, width), jnp.float32)
        second_shape = jax.ShapeDtypeStruct((hidden, filter_len), jnp.float32)
        scratch = [
            pltpu.VMEM((14, 2 * size, width), jnp.float32),
            pltpu.VMEM((2 * groups, 2 * size, width), jnp.bfloat16),
            pltpu.VMEM((2 * groups, 16, 128), jnp.float32),
        ]
        if last:
            operands += [
                mixer_weight,
                mixer_freq[:, None],
                embed_freq[:, None],
                features,
                first_pre,
                first_act,
                first_cos,
                second_pre,
                second_cos,
            ]
            out_shape = [part_shape, jax.ShapeDtypeStruct((hidden, 2 * hidden), jnp.float32)]
            scratch.append(pltpu.VMEM((hidden, filter_len), jnp.float32))
        else:
            out_shape = [part_shape, second_shape]
        part, out = pl.pallas_call(
            functools.partial(main_kernel, size, groups, filter_len, first, last),
            in_specs=[pl.BlockSpec(memory_space=pltpu.SMEM)]
            + [pl.BlockSpec(memory_space=pltpu.VMEM)] * (len(operands) - 1),
            out_specs=[pl.BlockSpec(memory_space=pltpu.VMEM)] * 2,
            out_shape=out_shape,
            scratch_shapes=scratch,
            compiler_params=pltpu.CompilerParams(vmem_limit_bytes=40 * 2**20),
            cost_estimate=pl.CostEstimate(
                flops=4 * 10**9, bytes_accessed=8 * 2**20, transcendentals=0
            ),
            name="filter_grad",
        )(*operands)
        parts.append(part)
        if last:
            net = out
        else:
            second_grad = out

    far_bits = bits_of("seq", 2)
    for bit in bits_of("chan"):
        net = net + swapped(net, "chan", bit)
    parts = [p + swapped(p, "seq", far_bits[0]) for p in parts]
    net, *parts = lax.optimization_barrier((net, *parts))
    for bit in far_bits:
        net = net + swapped(net, "seq", bit)
    for bit in far_bits[1:]:
        parts = [p + swapped(p, "seq", bit) for p in parts]
    net, *parts = lax.optimization_barrier((net, *parts))
    far = swapped(net, "seq", 1)
    both = []
    for p in parts:
        both += [p, swapped(p, "seq", 1)]

    feats = features.shape[0]
    row = jax.ShapeDtypeStruct((1, hidden), jnp.float32)
    outs = pl.pallas_call(
        functools.partial(finish_kernel, feats),
        in_specs=[pl.BlockSpec(memory_space=pltpu.SMEM)]
        + [pl.BlockSpec(memory_space=pltpu.VMEM)] * (2 + len(both)),
        out_specs=[pl.BlockSpec(memory_space=pltpu.VMEM)] * 8,
        out_shape=[
            jax.ShapeDtypeStruct((feats, hidden), jnp.float32),
            row,
            row,
            jax.ShapeDtypeStruct((hidden, hidden), jnp.float32),
            row,
            row,
            jax.ShapeDtypeStruct((hidden, chan_count), jnp.float32),
            jax.ShapeDtypeStruct((1, chan_count), jnp.float32),
        ],
        name="finish",
    )(par.reshape(1), net, far, *both)
    return tuple(o[0] if o.shape[0] == 1 else o for o in outs)


def solution(mesh):
    in_specs = (
        P("seq", "chan"),
        P("seq", "chan"),
        P(),
        P(),
        P(),
        P(),
        P(),
        P(),
        P(None, "chan"),
        P("chan"),
    )
    out_specs = (P(), P(), P(), P(), P(), P(), P(None, "chan"), P("chan"))
    return jax.shard_map(shards, mesh=mesh, in_specs=in_specs, out_specs=out_specs, check_vma=False)
```

```python
import functools
import math

import jax
import jax.numpy as jnp
import numpy as np
from jax import lax
from jax.experimental import pallas as pl
from jax.experimental.pallas import tpu as pltpu
from jax.sharding import PartitionSpec as P

BANDS = 8
SPAN_PARTS = 3
EXACT = lax.Precision.HIGHEST


def shifted(value, axis, steps):
    count = lax.axis_size(axis)
    first, last = (max(0, -steps), min(count, count - steps))
    return lax.ppermute(value, axis, [(source, source + steps) for source in range(first, last)])


def swapped(value, axis, bit):
    return lax.ppermute(value, axis, [(i, i ^ bit) for i in range(lax.axis_size(axis))])


def bits_of(axis, first=1):
    count = lax.axis_size(axis)
    assert count & (count - 1) == 0
    return [1 << i for i in range(count.bit_length() - 1) if (1 << i) >= first]


def split_const(matrix):
    high = matrix.astype(np.float32).astype(jnp.bfloat16)
    low = (matrix - high.astype(np.float64)).astype(np.float32).astype(jnp.bfloat16)
    return high, low


@functools.cache
def transforms(size):
    freqs = np.arange(0, size, 2)
    freqs = np.concatenate([freqs, size - 1 - freqs])
    omega = np.pi * (2 * freqs + 1) / (2 * size)
    steps = np.arange(size)
    forward = np.concatenate(
        [np.cos(omega[:, None] * steps), -np.sin(omega[:, None] * steps)], axis=0
    )
    omega = omega[: size // 2]
    dist = size - tap_order(size)
    inverse = (
        np.concatenate(
            [np.cos(dist[:, None] * omega), -np.sin(dist[:, None] * omega)], axis=1
        )
        / size
    )
    return split_const(forward), split_const(inverse)


def tap_order(size):
    return np.concatenate([np.arange(0, size, 2), np.arange(1, size, 2)])


def split_pair(value):
    high = value.astype(jnp.bfloat16)
    return high, (value - high.astype(jnp.float32)).astype(jnp.bfloat16)


@functools.cache
def tap_features(filter_len, size, band_count):
    tap = np.concatenate([m * size + tap_order(size) for m in range(filter_len // size)])
    scaled = tap.astype(np.float32) / np.float32(filter_len)
    rates = [max(1, filter_len // 4 // 2 ** (band_count - i)) for i in range(1, band_count + 1)]
    cycles = np.array(rates)[:, None] * tap[None, :] % filter_len
    angle = cycles.astype(np.float32) * np.float32(2.0 * math.pi / filter_len)
    angle = angle.astype(np.float64)
    return np.concatenate([scaled[None, :], np.cos(angle), np.sin(angle)], axis=0).astype(
        np.float32
    )


def dot32(left, right, dims=(((1,), (0,)), ((), ()))):
    return lax.dot_general(
        left, right, dims, precision=EXACT, preferred_element_type=jnp.float32
    )


def dot16(left, right, dims=(((1,), (0,)), ((), ()))):
    return lax.dot_general(left, right, dims, preferred_element_type=jnp.float32)


NT = (((1,), (1,)), ((), ()))
FIXED, BEYOND, WINDOWED = 0, 4, 6


def block_pairs(groups):
    return [(b, j, b + 4 - j) for j in range(8) for b in range(4) if 0 <= b + 4 - j < groups]


TN = (((0,), (0,)), ((), ()))


def prep_kernel(
    ew_ref,
    eb_ref,
    ef_ref,
    mw_ref,
    mb_ref,
    mf_ref,
    feats_ref,
    acth_ref,
    actl_ref,
    pre1_ref,
    act1_ref,
    cos1_ref,
    pre2_ref,
    cos2_ref,
    cols_ref,
):
    hidden = mw_ref.shape[0]
    vectors = jnp.concatenate(
        [eb_ref[...], ef_ref[...], mb_ref[...], mf_ref[...]] * 2, axis=0
    )
    vectors = jnp.concatenate([vectors, jnp.zeros_like(vectors)], axis=1).T
    cols_ref[...] = vectors[:hidden]
    first_pre = dot32(ew_ref[...], feats_ref[...], TN) + cols_ref[:, 0:1]
    angle = first_pre * cols_ref[:, 1:2]
    first_act = jnp.sin(angle)
    pre1_ref[...] = first_pre
    act1_ref[...] = first_act
    cos1_ref[...] = jnp.cos(angle)
    second_pre = dot32(mw_ref[...], first_act, TN) + cols_ref[:, 2:3]
    angle = second_pre * cols_ref[:, 3:4]
    second_act = jnp.sin(angle)
    pre2_ref[...] = second_pre
    cos2_ref[...] = jnp.cos(angle)
    for i, value in enumerate((second_act, second_act * feats_ref[0:1, :])):
        high, low = split_pair(value)
        acth_ref[i * hidden : (i + 1) * hidden, :] = high
        actl_ref[i * hidden : (i + 1) * hidden, :] = low


def main_kernel(
    size,
    groups,
    filter_len,
    first,
    last,
    chunk,
    par_ref,
    xk_ref,
    gk_ref,
    e1_ref,
    e2_ref,
    xp_ref,
    gn_ref,
    s3_ref,
    fwd_ref,
    inv_ref,
    acth_ref,
    actl_ref,
    head_ref,
    rates_ref,
    *rest,
):
    rest = list(rest)
    second_in = None if first else rest.pop(0)
    if last:
        net_in, rest = rest[:8], rest[8:]
        part_ref, net_ref, spec, prod, hold, second_ref = rest
    else:
        part_ref, second_ref, spec, prod, hold = rest
    par = par_ref[0]
    width = xk_ref.shape[1]
    hidden = head_ref.shape[0]
    mid = size // 2

    def transform(ref, slot):
        for i in range(2):
            block = ref[i * size : (i + 1) * size, :]
            spec[slot + (i ^ par)] = dot16(fwd_ref[par], jnp.concatenate([block, block], axis=0))

    half = head_ref.shape[1] // 2
    here = pl.ds(pl.multiple_of(par * half + chunk * width, width), width)

    transform(xk_ref, (WINDOWED + 4) * (1 - par))
    transform(gk_ref, (WINDOWED + 4) * par)
    transform(xp_ref, WINDOWED - 2 * par)
    transform(gn_ref, BEYOND + 2 * par)
    transform(e1_ref, WINDOWED + 6)
    transform(e2_ref, FIXED + 2)
    transform(s3_ref, WINDOWED + 2)

    lanes = 128
    rows = 16
    tiles = mid // rows

    def products(row, lane, sign):
        def load(slot):
            return (
                spec[slot, pl.ds(row, rows), pl.ds(lane, lanes)],
                spec[slot, pl.ds(row + size, rows), pl.ds(lane, lanes)],
            )

        acc_re = [None] * groups
        acc_im = [None] * groups

        def add(m, g, w):
            re = g[0] * w[0] + g[1] * w[1]
            im = g[0] * w[1] - g[1] * w[0]
            acc_re[m] = re if acc_re[m] is None else acc_re[m] + re
            acc_im[m] = im if acc_im[m] is None else acc_im[m] + im

        fixed = [load(FIXED + b) for b in range(4)]
        prev = None
        for j in range(8):
            now = load(WINDOWED + j)
            if prev is None:
                w = (now[1], -now[0]) if sign > 0 else (-now[1], now[0])
            elif sign > 0:
                w = (prev[0] + now[1], prev[1] - now[0])
            else:
                w = (prev[0] - now[1], prev[1] + now[0])
            for b, jj, m in block_pairs(groups):
                if jj == j:
                    add(m, fixed[b], w)
            if j == 3:
                near, far = load(BEYOND), load(BEYOND + 1)
                add(5, near, w)
                add(4, near, now)
                add(5, far, now)
            prev = now
        return acc_re, acc_im

    def body(it, carry):
        row = pl.multiple_of((it % tiles) * rows, rows)
        lane = pl.multiple_of((it // tiles) * lanes, lanes)
        even_re, even_im = products(row, lane, 1)
        for m in range(groups):
            hold[2 * m] = even_re[m]
            hold[2 * m + 1] = even_im[m]
        odd_re, odd_im = products(row + mid, lane, -1)
        for m in range(groups):
            re, im = hold[2 * m], hold[2 * m + 1]
            folded = (re + odd_re[m], im - odd_im[m], re - odd_re[m], im + odd_im[m])
            for part, value in enumerate(folded):
                high, low = split_pair(value)
                at = (pl.ds(row + part * mid, rows), pl.ds(lane, lanes))
                prod[2 * m, at[0], at[1]] = high
                prod[2 * m + 1, at[0], at[1]] = low
        return carry

    lax.fori_loop(0, tiles * (width // lanes), body, 0)

    rates = rates_ref[:, here]
    tap = lax.broadcasted_iota(jnp.int32, (size, width), 0)
    tap = jnp.where(tap < mid, 2 * tap, 2 * (tap - mid) + 1)
    inner = jnp.exp(-(tap.astype(jnp.float32) / filter_len) * rates)
    head = head_ref[:, here]
    head_high, head_low = split_pair(head)
    total = jnp.zeros((2 * hidden, width), jnp.float32)
    for m in range(groups):
        grads = []
        for q in range(2):
            high = prod[2 * m, q * size : (q + 1) * size, :]
            low = prod[2 * m + 1, q * size : (q + 1) * size, :]
            both = dot16(inv_ref[q], high)
            grads.append(both[:mid] + both[mid:] + dot16(inv_ref[q, :mid, :], low))
        outer = jnp.exp(-(m * size / filter_len) * rates)
        delta = jnp.concatenate(grads, axis=0) * (inner * outer)
        high, low = split_pair(delta)
        cols = slice(m * size, (m + 1) * size)
        total += (
            dot16(acth_ref[:, cols], high)
            + dot16(acth_ref[:, cols], low)
            + dot16(actl_ref[:, cols], high)
        )
        second = (
            dot16(head_high, high, NT) + dot16(head_high, low, NT) + dot16(head_low, high, NT)
        )
        second_ref[:, cols] = second if first else second + second_in[:, cols]

    part_ref[:hidden, :] = total[:hidden]
    part_ref[hidden:, :] = jnp.broadcast_to(
        -jnp.sum(total[hidden:] * head, axis=0, keepdims=True),
        (part_ref.shape[0] - hidden, width),
    )

    if last:
        mix, cols, feats, pre1, act1, cos1, pre2, cos2 = (r[...] for r in net_in)
        mix_freq, emb_freq = cols[:, 3:4], cols[:, 1:2]
        slope2 = second_ref[...] * cos2
        delta2 = slope2 * mix_freq
        slope1 = dot32(mix, delta2) * cos1
        delta1 = slope1 * emb_freq
        count = feats.shape[0]
        net_ref[:, :hidden] = dot32(delta2, act1, NT)
        net_ref[:, hidden : hidden + count] = dot32(delta1, feats, NT)
        for i, value in enumerate((delta1, slope1 * pre1, delta2, slope2 * pre2)):
            at = hidden + count + i
            net_ref[:, at : at + 1] = jnp.sum(value, axis=1, keepdims=True)
        at = hidden + count + 4
        net_ref[:, at:] = jnp.zeros((hidden, net_ref.shape[1] - at), jnp.float32)


def finish_kernel(count, par_ref, net_ref, far_ref, *rest):
    ew_ref, eb_ref, ef_ref, mw_ref, mb_ref, mf_ref, head_ref, rates_ref = rest[-8:]
    parts = rest[:-8]
    par = par_ref[0]
    turned = (net_ref[...] + far_ref[...]).T
    hidden = turned.shape[1]
    mw_ref[...] = turned[:hidden]
    ew_ref[...] = turned[hidden : hidden + count]
    for i, ref in enumerate((eb_ref, ef_ref, mb_ref, mf_ref)):
        ref[...] = turned[hidden + count + i : hidden + count + i + 1]
    width = parts[0].shape[1]
    half = head_ref.shape[1] // 2
    for i in range(len(parts) // 2):
        for which, ref in ((par, parts[2 * i]), (1 - par, parts[2 * i + 1])):
            at = pl.ds(pl.multiple_of(which * half + i * width, width), width)
            head_ref[:, at] = ref[:hidden, :]
            rates_ref[:, at] = ref[hidden : hidden + 1, :]


def after(value, *others):
    return lax.optimization_barrier((value, *others))[0]


def shards(
    inputs,
    out_grad,
    embed_weight,
    embed_bias,
    embed_freq,
    mixer_weight,
    mixer_bias,
    mixer_freq,
    head_weight,
    decay_rates,
):
    block_len, chan_count = inputs.shape
    hidden = head_weight.shape[0]
    half = chan_count // 2
    size = block_len // 2
    filter_len = SPAN_PARTS * block_len
    groups = filter_len // size
    par = lax.axis_index("seq") % 2
    count = lax.axis_size("seq")
    width = min(256, half)
    chunks = range(half // width)

    def part_of(value, which, chunk, span):
        start = which * half + chunk * span
        return lax.dynamic_slice_in_dim(value, start, span, axis=1)

    def gives(chunk):
        x_give = part_of(inputs, 1 - par, chunk, width)
        g_give = part_of(out_grad, 1 - par, chunk, width)
        return jnp.where(par == 0, g_give, x_give), jnp.where(par == 0, x_give, g_give)

    ahead = [(i, i + 2) for i in range(0, count - 2, 2)]
    back = [(i, i - 2) for i in range(3, count, 2)]
    one, two = zip(*[gives(c) for c in chunks])
    one, two = list(one), list(two)
    e1, e2, s3 = [], [], []
    e1.append(swapped(one[0], "seq", 1))
    x_keep = part_of(inputs, par, 0, half)
    g_keep = part_of(out_grad, par, 0, half)
    x_prev = shifted(x_keep, "seq", 2)
    g_next = shifted(after(g_keep, e1[0]), "seq", -2)
    for c in chunks[1:]:
        e1.append(swapped(after(one[c], e1[-1]), "seq", 1))
        s3.append(lax.ppermute(e1[-2], "seq", ahead + back))
    s3.append(lax.ppermute(e1[-1], "seq", ahead + back))
    for c in chunks:
        e2.append(swapped(after(two[c], e1[-1] if c == 0 else e2[-1]), "seq", 1))

    features = jnp.asarray(tap_features(filter_len, size, BANDS))
    feats = features.shape[0]
    taps = jax.ShapeDtypeStruct((hidden, filter_len), jnp.float32)
    wide = jax.ShapeDtypeStruct((2 * hidden, filter_len), jnp.bfloat16)
    vmem = pl.BlockSpec(memory_space=pltpu.VMEM)
    act_high, act_low, first_pre, first_act, first_cos, second_pre, second_cos, cols = (
        pl.pallas_call(
            prep_kernel,
            in_specs=[vmem] * 7,
            out_specs=[vmem] * 8,
            out_shape=[wide, wide] + [taps] * 5 + [jax.ShapeDtypeStruct((hidden, 8), jnp.float32)],
            name="prep",
        )(
            after(embed_weight, e1[0]),
            embed_bias[None, :],
            embed_freq[None, :],
            mixer_weight,
            mixer_bias[None, :],
            mixer_freq[None, :],
            features,
        )
    )

    (fwd_high, fwd_low), (inv_high, inv_low) = transforms(size)
    forward = np.concatenate([fwd_high, fwd_low], axis=1)
    mirrored = np.concatenate([forward[:size], -forward[size:]], axis=0)
    forward = jnp.asarray(np.stack([forward, mirrored]))
    mid = size // 2
    inverse = jnp.asarray(
        np.stack(
            [
                np.concatenate([inv_high[q * mid : (q + 1) * mid], inv_low[q * mid : (q + 1) * mid]])
                for q in range(2)
            ]
        )
    )

    parts = []
    second_grad = None
    for c in chunks:
        first, last = c == 0, c == chunks[-1]
        here = slice(c * width, (c + 1) * width)
        operands = [
            par.reshape(1),
            x_keep[:, here],
            g_keep[:, here],
            e1[c],
            e2[c],
            x_prev[:, here],
            g_next[:, here],
            s3[c],
            forward,
            inverse,
            act_high,
            act_low,
            head_weight,
            decay_rates[None, :],
        ]
        if not first:
            operands.append(second_grad)
        part_shape = jax.ShapeDtypeStruct((hidden + 8, width), jnp.float32)
        second_shape = jax.ShapeDtypeStruct((hidden, filter_len), jnp.float32)
        scratch = [
            pltpu.VMEM((14, 2 * size, width), jnp.float32),
            pltpu.VMEM((2 * groups, 2 * size, width), jnp.bfloat16),
            pltpu.VMEM((2 * groups, 16, 128), jnp.float32),
        ]
        if last:
            operands += [
                mixer_weight,
                cols,
                features,
                first_pre,
                first_act,
                first_cos,
                second_pre,
                second_cos,
            ]
            out_shape = [part_shape, jax.ShapeDtypeStruct((hidden, 2 * hidden), jnp.float32)]
            scratch.append(pltpu.VMEM((hidden, filter_len), jnp.float32))
        else:
            out_shape = [part_shape, second_shape]
        part, out = pl.pallas_call(
            functools.partial(main_kernel, size, groups, filter_len, first, last, c),
            in_specs=[pl.BlockSpec(memory_space=pltpu.SMEM)]
            + [pl.BlockSpec(memory_space=pltpu.VMEM)] * (len(operands) - 1),
            out_specs=[pl.BlockSpec(memory_space=pltpu.VMEM)] * 2,
            out_shape=out_shape,
            scratch_shapes=scratch,
            compiler_params=pltpu.CompilerParams(vmem_limit_bytes=40 * 2**20),
            cost_estimate=pl.CostEstimate(
                flops=4 * 10**9, bytes_accessed=8 * 2**20, transcendentals=0
            ),
            name="filter_grad",
        )(*operands)
        parts.append(part)
        if last:
            net = out
        else:
            second_grad = out

    far_bits = bits_of("seq", 2)
    for bit in bits_of("chan"):
        net = net + swapped(net, "chan", bit)
    parts = [p + swapped(p, "seq", far_bits[0]) for p in parts]
    net, *parts = lax.optimization_barrier((net, *parts))
    for bit in far_bits:
        net = net + swapped(net, "seq", bit)
    for bit in far_bits[1:]:
        parts = [p + swapped(p, "seq", bit) for p in parts]
    net, *parts = lax.optimization_barrier((net, *parts))
    far = swapped(net, "seq", 1)
    both = []
    for p in parts:
        both += [p, swapped(p, "seq", 1)]

    row = jax.ShapeDtypeStruct((1, hidden), jnp.float32)
    outs = pl.pallas_call(
        functools.partial(finish_kernel, feats),
        in_specs=[pl.BlockSpec(memory_space=pltpu.SMEM)]
        + [pl.BlockSpec(memory_space=pltpu.VMEM)] * (2 + len(both)),
        out_specs=[pl.BlockSpec(memory_space=pltpu.VMEM)] * 8,
        out_shape=[
            jax.ShapeDtypeStruct((feats, hidden), jnp.float32),
            row,
            row,
            jax.ShapeDtypeStruct((hidden, hidden), jnp.float32),
            row,
            row,
            jax.ShapeDtypeStruct((hidden, chan_count), jnp.float32),
            jax.ShapeDtypeStruct((1, chan_count), jnp.float32),
        ],
        name="finish",
    )(par.reshape(1), net, far, *both)
    return tuple(o[0] if o.shape[0] == 1 else o for o in outs)


def solution(mesh):
    in_specs = (
        P("seq", "chan"),
        P("seq", "chan"),
        P(),
        P(),
        P(),
        P(),
        P(),
        P(),
        P(None, "chan"),
        P("chan"),
    )
    out_specs = (P(), P(), P(), P(), P(), P(), P(None, "chan"), P("chan"))
    return jax.shard_map(shards, mesh=mesh, in_specs=in_specs, out_specs=out_specs, check_vma=False)
```

```python
import functools
import math

import jax
import jax.numpy as jnp
import numpy as np
from jax import lax
from jax.experimental import pallas as pl
from jax.experimental.pallas import tpu as pltpu
from jax.sharding import PartitionSpec as P


BANDS = 8
SPAN_PARTS = 3
EXACT = lax.Precision.HIGHEST


def swapped(value, axis, bit):
    return lax.ppermute(value, axis, [(i, i ^ bit) for i in range(lax.axis_size(axis))])


def bits_of(axis, first=1):
    count = lax.axis_size(axis)
    assert count & (count - 1) == 0
    return [1 << i for i in range(count.bit_length() - 1) if (1 << i) >= first]


def split_const(matrix):
    high = matrix.astype(np.float32).astype(jnp.bfloat16)
    low = (matrix - high.astype(np.float64)).astype(np.float32).astype(jnp.bfloat16)
    return high, low


@functools.cache
def transforms(size):
    freqs = np.arange(0, size, 2)
    freqs = np.concatenate([freqs, size - 1 - freqs])
    omega = np.pi * (2 * freqs + 1) / (2 * size)
    steps = np.arange(size)
    forward = np.concatenate(
        [np.cos(omega[:, None] * steps), -np.sin(omega[:, None] * steps)], axis=0
    )
    omega = omega[: size // 2]
    dist = size - tap_order(size)
    inverse = (
        np.concatenate(
            [np.cos(dist[:, None] * omega), -np.sin(dist[:, None] * omega)], axis=1
        )
        / size
    )
    return split_const(forward), split_const(inverse)


def tap_order(size):
    return np.concatenate([np.arange(0, size, 2), np.arange(1, size, 2)])


def split_pair(value):
    high = value.astype(jnp.bfloat16)
    return high, (value - high.astype(jnp.float32)).astype(jnp.bfloat16)


@functools.cache
def tap_features(filter_len, size, band_count):
    tap = np.concatenate([m * size + tap_order(size) for m in range(filter_len // size)])
    scaled = tap.astype(np.float32) / np.float32(filter_len)
    rates = [max(1, filter_len // 4 // 2 ** (band_count - i)) for i in range(1, band_count + 1)]
    cycles = np.array(rates)[:, None] * tap[None, :] % filter_len
    angle = cycles.astype(np.float32) * np.float32(2.0 * math.pi / filter_len)
    angle = angle.astype(np.float64)
    return np.concatenate([scaled[None, :], np.cos(angle), np.sin(angle)], axis=0).astype(
        np.float32
    )


def dot32(left, right, dims=(((1,), (0,)), ((), ()))):
    return lax.dot_general(
        left, right, dims, precision=EXACT, preferred_element_type=jnp.float32
    )


def dot16(left, right, dims=(((1,), (0,)), ((), ()))):
    return lax.dot_general(left, right, dims, preferred_element_type=jnp.float32)


NT = (((1,), (1,)), ((), ()))
FIXED, BEYOND, WINDOWED = 0, 4, 6


def block_pairs(groups):
    return [(b, j, b + 4 - j) for j in range(8) for b in range(4) if 0 <= b + 4 - j < groups]


TN = (((0,), (0,)), ((), ()))
SIN_TERMS = [(-1.0) ** i / math.factorial(2 * i + 1) for i in range(6)]
COS_TERMS = [(-1.0) ** i / math.factorial(2 * i) for i in range(7)]


def sine_cosine(angle):
    turns = jnp.floor(angle * (1.0 / math.pi) + 0.5)
    rest = angle - turns * 3.140625
    rest = rest - turns * 9.67502593994140625e-4
    rest = rest - turns * 1.509957990978376432e-7
    sign = 1.0 - 4.0 * (0.5 * turns - jnp.floor(0.5 * turns))
    square = rest * rest
    sine = SIN_TERMS[-1]
    for term in SIN_TERMS[-2::-1]:
        sine = sine * square + term
    cosine = COS_TERMS[-1]
    for term in COS_TERMS[-2::-1]:
        cosine = cosine * square + term
    return sine * (rest * sign), cosine * sign


def prep_kernel(
    ew_ref,
    eb_ref,
    ef_ref,
    mw_ref,
    mb_ref,
    mf_ref,
    feats_ref,
    acth_ref,
    actl_ref,
    pre1_ref,
    act1_ref,
    cos1_ref,
    pre2_ref,
    cos2_ref,
    cols_ref,
):
    hidden = mw_ref.shape[0]
    vectors = jnp.concatenate(
        [eb_ref[...], ef_ref[...], mb_ref[...], mf_ref[...]] * 2, axis=0
    )
    vectors = jnp.concatenate([vectors, jnp.zeros_like(vectors)], axis=1).T
    cols_ref[...] = vectors[:hidden]
    first_pre = dot32(ew_ref[...], feats_ref[...], TN) + cols_ref[:, 0:1]
    first_act, first_cos = sine_cosine(first_pre * cols_ref[:, 1:2])
    pre1_ref[...] = first_pre
    act1_ref[...] = first_act
    cos1_ref[...] = first_cos
    second_pre = dot32(mw_ref[...], first_act, TN) + cols_ref[:, 2:3]
    second_act, second_cos = sine_cosine(second_pre * cols_ref[:, 3:4])
    pre2_ref[...] = second_pre
    cos2_ref[...] = second_cos
    for i, value in enumerate((second_act, second_act * feats_ref[0:1, :])):
        high, low = split_pair(value)
        acth_ref[i * hidden : (i + 1) * hidden, :] = high
        actl_ref[i * hidden : (i + 1) * hidden, :] = low


def main_kernel(
    size,
    groups,
    filter_len,
    first,
    last,
    chunk,
    par_ref,
    xk_ref,
    gk_ref,
    e1_ref,
    e2_ref,
    za_ref,
    zb_ref,
    s3_ref,
    fwd_ref,
    inv_ref,
    acth_ref,
    actl_ref,
    head_ref,
    rates_ref,
    *rest,
):
    rest = list(rest)
    second_in = None if first else rest.pop(0)
    if last:
        net_in, rest = rest[:8], rest[8:]
        part_ref, net_ref, spec, prod, hold, second_ref = rest
    else:
        part_ref, second_ref, spec, prod, hold = rest
    par = par_ref[0]
    width = xk_ref.shape[1]
    hidden = head_ref.shape[0]
    mid = size // 2

    def transform(ref, slot):
        for i in range(2):
            block = ref[i * size : (i + 1) * size, :]
            spec[slot + (i ^ par)] = dot16(fwd_ref[par], jnp.concatenate([block, block], axis=0))

    half = head_ref.shape[1] // 2
    here = pl.ds(pl.multiple_of(par * half + chunk * width, width), width)

    transform(xk_ref, (WINDOWED + 4) * (1 - par))
    transform(gk_ref, (WINDOWED + 4) * par)
    before, beyond = WINDOWED - 2 * par, BEYOND + 2 * par
    odd = par_ref[1]
    transform(za_ref, beyond + odd * (before - beyond))
    transform(zb_ref, before + odd * (beyond - before))
    transform(e1_ref, WINDOWED + 6)
    transform(e2_ref, FIXED + 2)
    transform(s3_ref, WINDOWED + 2)

    lanes = 128
    rows = 16
    tiles = mid // rows

    def products(row, lane, sign):
        def load(slot):
            return (
                spec[slot, pl.ds(row, rows), pl.ds(lane, lanes)],
                spec[slot, pl.ds(row + size, rows), pl.ds(lane, lanes)],
            )

        acc_re = [None] * groups
        acc_im = [None] * groups

        def add(m, g, w):
            re = g[0] * w[0] + g[1] * w[1]
            im = g[0] * w[1] - g[1] * w[0]
            acc_re[m] = re if acc_re[m] is None else acc_re[m] + re
            acc_im[m] = im if acc_im[m] is None else acc_im[m] + im

        fixed = [load(FIXED + b) for b in range(4)]
        prev = None
        for j in range(8):
            now = load(WINDOWED + j)
            if prev is None:
                w = (now[1], -now[0]) if sign > 0 else (-now[1], now[0])
            elif sign > 0:
                w = (prev[0] + now[1], prev[1] - now[0])
            else:
                w = (prev[0] - now[1], prev[1] + now[0])
            for b, jj, m in block_pairs(groups):
                if jj == j:
                    add(m, fixed[b], w)
            if j == 3:
                near, far = load(BEYOND), load(BEYOND + 1)
                add(5, near, w)
                add(4, near, now)
                add(5, far, now)
            prev = now
        return acc_re, acc_im

    def body(it, carry):
        row = pl.multiple_of((it % tiles) * rows, rows)
        lane = pl.multiple_of((it // tiles) * lanes, lanes)
        even_re, even_im = products(row, lane, 1)
        for m in range(groups):
            hold[2 * m] = even_re[m]
            hold[2 * m + 1] = even_im[m]
        odd_re, odd_im = products(row + mid, lane, -1)
        for m in range(groups):
            re, im = hold[2 * m], hold[2 * m + 1]
            folded = (re + odd_re[m], im - odd_im[m], re - odd_re[m], im + odd_im[m])
            for part, value in enumerate(folded):
                high, low = split_pair(value)
                at = (pl.ds(row + part * mid, rows), pl.ds(lane, lanes))
                prod[2 * m, at[0], at[1]] = high
                prod[2 * m + 1, at[0], at[1]] = low
        return carry

    lax.fori_loop(0, tiles * (width // lanes), body, 0)

    rates = rates_ref[:, here]
    tap = lax.broadcasted_iota(jnp.int32, (size, width), 0)
    tap = jnp.where(tap < mid, 2 * tap, 2 * (tap - mid) + 1)
    inner = jnp.exp(-(tap.astype(jnp.float32) / filter_len) * rates)
    head = head_ref[:, here]
    head_high, head_low = split_pair(head)
    total = jnp.zeros((2 * hidden, width), jnp.float32)
    for m in range(groups):
        grads = []
        for q in range(2):
            high = prod[2 * m, q * size : (q + 1) * size, :]
            low = prod[2 * m + 1, q * size : (q + 1) * size, :]
            both = dot16(inv_ref[q], high)
            grads.append(both[:mid] + both[mid:] + dot16(inv_ref[q, :mid, :], low))
        outer = jnp.exp(-(m * size / filter_len) * rates)
        delta = jnp.concatenate(grads, axis=0) * (inner * outer)
        high, low = split_pair(delta)
        cols = slice(m * size, (m + 1) * size)
        total += (
            dot16(acth_ref[:, cols], high)
            + dot16(acth_ref[:, cols], low)
            + dot16(actl_ref[:, cols], high)
        )
        second = (
            dot16(head_high, high, NT) + dot16(head_high, low, NT) + dot16(head_low, high, NT)
        )
        second_ref[:, cols] = second if first else second + second_in[:, cols]

    part_ref[:hidden, :] = total[:hidden]
    part_ref[hidden:, :] = jnp.broadcast_to(
        -jnp.sum(total[hidden:] * head, axis=0, keepdims=True),
        (part_ref.shape[0] - hidden, width),
    )

    if last:
        mix, cols, feats, pre1, act1, cos1, pre2, cos2 = (r[...] for r in net_in)
        mix_freq, emb_freq = cols[:, 3:4], cols[:, 1:2]
        slope2 = second_ref[...] * cos2
        delta2 = slope2 * mix_freq
        slope1 = dot32(mix, delta2) * cos1
        delta1 = slope1 * emb_freq
        count = feats.shape[0]
        net_ref[:, :hidden] = dot32(delta2, act1, NT)
        net_ref[:, hidden : hidden + count] = dot32(delta1, feats, NT)
        for i, value in enumerate((delta1, slope1 * pre1, delta2, slope2 * pre2)):
            at = hidden + count + i
            net_ref[:, at : at + 1] = jnp.sum(value, axis=1, keepdims=True)
        at = hidden + count + 4
        net_ref[:, at:] = jnp.zeros((hidden, net_ref.shape[1] - at), jnp.float32)


def finish_kernel(count, par_ref, net_ref, far_ref, *rest):
    ew_ref, eb_ref, ef_ref, mw_ref, mb_ref, mf_ref, head_ref, rates_ref = rest[-8:]
    parts = rest[:-8]
    par = par_ref[0]
    turned = (net_ref[...] + far_ref[...]).T
    hidden = turned.shape[1]
    mw_ref[...] = turned[:hidden]
    ew_ref[...] = turned[hidden : hidden + count]
    for i, ref in enumerate((eb_ref, ef_ref, mb_ref, mf_ref)):
        ref[...] = turned[hidden + count + i : hidden + count + i + 1]
    width = parts[0].shape[1]
    half = head_ref.shape[1] // 2
    for i in range(len(parts) // 2):
        for which, ref in ((par, parts[2 * i]), (1 - par, parts[2 * i + 1])):
            at = pl.ds(pl.multiple_of(which * half + i * width, width), width)
            head_ref[:, at] = ref[:hidden, :]
            rates_ref[:, at] = ref[hidden : hidden + 1, :]


def after(value, *others):
    return lax.optimization_barrier((value, *others))[0]


def work(
    inputs,
    out_grad,
    embed_weight,
    embed_bias,
    embed_freq,
    mixer_weight,
    mixer_bias,
    mixer_freq,
    head_weight,
    decay_rates,
):
    block_len, chan_count = inputs.shape
    hidden = head_weight.shape[0]
    half = chan_count // 2
    size = block_len // 2
    filter_len = SPAN_PARTS * block_len
    groups = filter_len // size
    par = lax.axis_index("seq") % 2
    count = lax.axis_size("seq")
    width = min(256, half)
    chunks = range(half // width)

    def part_of(value, which, chunk, span):
        start = which * half + chunk * span
        return lax.dynamic_slice_in_dim(value, start, span, axis=1)

    def gives(inputs, out_grad, chunk):
        x_give = part_of(inputs, 1 - par, chunk, width)
        g_give = part_of(out_grad, 1 - par, chunk, width)
        return jnp.where(par == 0, g_give, x_give), jnp.where(par == 0, x_give, g_give)

    odd = (lax.axis_index("seq") // 2) % 2
    place = jnp.stack([par, odd]).astype(jnp.int32)
    ahead = [(i, i + 2) for i in range(0, count - 2, 2)]
    back = [(i, i - 2) for i in range(3, count, 2)]
    upper = [i for i in range(count - 2) if (i // 2) % 2 == 1]
    middle = [(i, i + 2) for i in upper] + [(i + 2, i) for i in upper]
    one0, _ = gives(inputs, out_grad, 0)
    e1 = [swapped(one0, "seq", 1)]
    own_in, own_grad, _ = lax.optimization_barrier((inputs, out_grad, one0))
    x_keep = part_of(own_in, par, 0, half)
    g_keep = part_of(own_grad, par, 0, half)
    za = swapped(jnp.where(odd == 0, x_keep, g_keep), "seq", 2)
    zb = lax.ppermute(jnp.where(odd == 0, g_keep, x_keep), "seq", middle)
    own_in, own_grad, _ = lax.optimization_barrier((own_in, own_grad, x_keep))
    sends = [gives(own_in, own_grad, c) for c in chunks]
    e2, s3 = [], []
    for c in chunks[1:]:
        e1.append(swapped(after(sends[c][0], e1[-1]), "seq", 1))
    for c in chunks:
        s3.append(lax.ppermute(e1[c], "seq", ahead + back))
    for c in chunks:
        e2.append(swapped(after(sends[c][1], e1[-1] if c == 0 else e2[-1]), "seq", 1))

    features = jnp.asarray(tap_features(filter_len, size, BANDS))
    feats = features.shape[0]
    taps = jax.ShapeDtypeStruct((hidden, filter_len), jnp.float32)
    wide = jax.ShapeDtypeStruct((2 * hidden, filter_len), jnp.bfloat16)
    vmem = pl.BlockSpec(memory_space=pltpu.VMEM)
    made = pl.pallas_call(
        prep_kernel,
        in_specs=[vmem] * 7,
        out_specs=[vmem] * 8,
        out_shape=[wide, wide] + [taps] * 5 + [jax.ShapeDtypeStruct((hidden, 8), jnp.float32)],
        name="prep",
    )(
        after(embed_weight, e1[0]),
        embed_bias[None, :],
        embed_freq[None, :],
        mixer_weight,
        mixer_bias[None, :],
        mixer_freq[None, :],
        features,
    )
    act_high, act_low, first_pre, first_act, first_cos, second_pre, second_cos, cols = made

    (fwd_high, fwd_low), (inv_high, inv_low) = transforms(size)
    forward = np.concatenate([fwd_high, fwd_low], axis=1)
    mirrored = np.concatenate([forward[:size], -forward[size:]], axis=0)
    forward = jnp.asarray(np.stack([forward, mirrored]))
    mid = size // 2
    inverse = jnp.asarray(
        np.stack(
            [
                np.concatenate([inv_high[q * mid : (q + 1) * mid], inv_low[q * mid : (q + 1) * mid]])
                for q in range(2)
            ]
        )
    )

    parts = []
    second_grad = None
    for c in chunks:
        first, last = c == 0, c == chunks[-1]
        here = slice(c * width, (c + 1) * width)
        operands = [
            place,
            x_keep[:, here],
            g_keep[:, here],
            e1[c],
            e2[c],
            za[:, here],
            zb[:, here],
            s3[c],
            forward,
            inverse,
            act_high,
            act_low,
            head_weight,
            decay_rates[None, :],
        ]
        if not first:
            operands.append(second_grad)
        part_shape = jax.ShapeDtypeStruct((hidden + 8, width), jnp.float32)
        second_shape = jax.ShapeDtypeStruct((hidden, filter_len), jnp.float32)
        scratch = [
            pltpu.VMEM((14, 2 * size, width), jnp.float32),
            pltpu.VMEM((2 * groups, 2 * size, width), jnp.bfloat16),
            pltpu.VMEM((2 * groups, 16, 128), jnp.float32),
        ]
        if last:
            operands += [
                mixer_weight,
                cols,
                features,
                first_pre,
                first_act,
                first_cos,
                second_pre,
                second_cos,
            ]
            out_shape = [part_shape, jax.ShapeDtypeStruct((hidden, 2 * hidden), jnp.float32)]
            scratch.append(pltpu.VMEM((hidden, filter_len), jnp.float32))
        else:
            out_shape = [part_shape, second_shape]
        part, out = pl.pallas_call(
            functools.partial(main_kernel, size, groups, filter_len, first, last, c),
            in_specs=[pl.BlockSpec(memory_space=pltpu.SMEM)]
            + [pl.BlockSpec(memory_space=pltpu.VMEM)] * (len(operands) - 1),
            out_specs=[pl.BlockSpec(memory_space=pltpu.VMEM)] * 2,
            out_shape=out_shape,
            scratch_shapes=scratch,
            compiler_params=pltpu.CompilerParams(vmem_limit_bytes=40 * 2**20),
            cost_estimate=pl.CostEstimate(
                flops=4 * 10**9, bytes_accessed=8 * 2**20, transcendentals=0
            ),
            name="filter_grad",
        )(*operands)
        parts.append(part)
        if last:
            net = out
        else:
            second_grad = out

    far_bits = bits_of("seq", 2)
    steps = [("chan", b) for b in bits_of("chan")] + [("seq", b) for b in far_bits]
    for axis, bit in steps:
        net = net + swapped(net, axis, bit)
    far = swapped(net, "seq", 1)
    both = []
    for p in parts:
        for bit in far_bits:
            p = p + swapped(p, "seq", bit)
        both += [p, swapped(p, "seq", 1)]

    row = jax.ShapeDtypeStruct((1, hidden), jnp.float32)
    outs = pl.pallas_call(
        functools.partial(finish_kernel, feats),
        in_specs=[pl.BlockSpec(memory_space=pltpu.SMEM)]
        + [pl.BlockSpec(memory_space=pltpu.VMEM)] * (2 + len(both)),
        out_specs=[pl.BlockSpec(memory_space=pltpu.VMEM)] * 8,
        out_shape=[
            jax.ShapeDtypeStruct((feats, hidden), jnp.float32),
            row,
            row,
            jax.ShapeDtypeStruct((hidden, hidden), jnp.float32),
            row,
            row,
            jax.ShapeDtypeStruct((hidden, chan_count), jnp.float32),
            jax.ShapeDtypeStruct((1, chan_count), jnp.float32),
        ],
        name="finish",
    )(place, net, far, *both)
    return tuple(o[0] if o.shape[0] == 1 else o for o in outs)


def solution(mesh):
    in_specs = (
        P("seq", "chan"),
        P("seq", "chan"),
        P(),
        P(),
        P(),
        P(),
        P(),
        P(),
        P(None, "chan"),
        P("chan"),
    )
    out_specs = (P(), P(), P(), P(), P(), P(), P(None, "chan"), P("chan"))
    return jax.shard_map(work, mesh=mesh, in_specs=in_specs, out_specs=out_specs, check_vma=False)
```

```python
import functools
import math

import jax
import jax.numpy as jnp
import numpy as np
from jax import lax
from jax.experimental import pallas as pl
from jax.experimental.pallas import tpu as pltpu
from jax.sharding import PartitionSpec as P


BANDS = 8
SPAN_PARTS = 3


def swapped(value, axis, bit):
    return lax.ppermute(value, axis, [(i, i ^ bit) for i in range(lax.axis_size(axis))])


def bits_of(axis, first=1):
    count = lax.axis_size(axis)
    assert count & (count - 1) == 0
    return [1 << i for i in range(count.bit_length() - 1) if (1 << i) >= first]


def split_const(matrix):
    high = matrix.astype(np.float32).astype(jnp.bfloat16)
    low = (matrix - high.astype(np.float64)).astype(np.float32).astype(jnp.bfloat16)
    return high, low


@functools.cache
def transforms(size):
    freqs = np.arange(0, size, 2)
    freqs = np.concatenate([freqs, size - 1 - freqs])
    omega = np.pi * (2 * freqs + 1) / (2 * size)
    steps = np.arange(size)
    forward = np.concatenate(
        [np.cos(omega[:, None] * steps), -np.sin(omega[:, None] * steps)], axis=0
    )
    omega = omega[: size // 2]
    dist = size - tap_order(size)
    inverse = (
        np.concatenate(
            [np.cos(dist[:, None] * omega), -np.sin(dist[:, None] * omega)], axis=1
        )
        / size
    )
    return split_const(forward), split_const(inverse)


def tap_order(size):
    return np.concatenate([np.arange(0, size, 2), np.arange(1, size, 2)])


def split_pair(value):
    high = value.astype(jnp.bfloat16)
    return high, (value - high.astype(jnp.float32)).astype(jnp.bfloat16)


@functools.cache
def tap_features(filter_len, size, band_count):
    tap = np.concatenate([m * size + tap_order(size) for m in range(filter_len // size)])
    scaled = tap.astype(np.float32) / np.float32(filter_len)
    rates = [max(1, filter_len // 4 // 2 ** (band_count - i)) for i in range(1, band_count + 1)]
    cycles = np.array(rates)[:, None] * tap[None, :] % filter_len
    angle = cycles.astype(np.float32) * np.float32(2.0 * math.pi / filter_len)
    angle = angle.astype(np.float64)
    return np.concatenate([scaled[None, :], np.cos(angle), np.sin(angle)], axis=0).astype(
        np.float32
    )


def dot16(left, right, dims=(((1,), (0,)), ((), ()))):
    return lax.dot_general(left, right, dims, preferred_element_type=jnp.float32)


def dot32(left, right, dims=(((1,), (0,)), ((), ()))):
    left_high, left_low = split_pair(left)
    right_high, right_low = split_pair(right)
    return (
        dot16(left_high, right_high, dims)
        + dot16(left_high, right_low, dims)
        + dot16(left_low, right_high, dims)
    )


NT = (((1,), (1,)), ((), ()))
FIXED, BEYOND, WINDOWED = 0, 4, 6


def block_pairs(groups):
    return [(b, j, b + 4 - j) for j in range(8) for b in range(4) if 0 <= b + 4 - j < groups]


TN = (((0,), (0,)), ((), ()))
SIN_TERMS = [(-1.0) ** i / math.factorial(2 * i + 1) for i in range(6)]
COS_TERMS = [(-1.0) ** i / math.factorial(2 * i) for i in range(7)]


def sine_cosine(angle):
    turns = jnp.floor(angle * (1.0 / math.pi) + 0.5)
    rest = angle - turns * 3.140625
    rest = rest - turns * 9.67502593994140625e-4
    rest = rest - turns * 1.509957990978376432e-7
    sign = 1.0 - 4.0 * (0.5 * turns - jnp.floor(0.5 * turns))
    square = rest * rest
    sine = SIN_TERMS[-1]
    for term in SIN_TERMS[-2::-1]:
        sine = sine * square + term
    cosine = COS_TERMS[-1]
    for term in COS_TERMS[-2::-1]:
        cosine = cosine * square + term
    return sine * (rest * sign), cosine * sign


def prep_kernel(
    ew_ref,
    eb_ref,
    ef_ref,
    mw_ref,
    mb_ref,
    mf_ref,
    feats_ref,
    act_ref,
    pre1_ref,
    act1_ref,
    cos1_ref,
    pre2_ref,
    cos2_ref,
    cols_ref,
):
    hidden = mw_ref.shape[0]
    vectors = jnp.concatenate(
        [eb_ref[...], ef_ref[...], mb_ref[...], mf_ref[...]] * 2, axis=0
    )
    vectors = jnp.concatenate([vectors, jnp.zeros_like(vectors)], axis=1).T
    cols_ref[...] = vectors[:hidden]
    first_pre = dot32(ew_ref[...], feats_ref[...], TN) + cols_ref[:, 0:1]
    first_act, first_cos = sine_cosine(first_pre * cols_ref[:, 1:2])
    pre1_ref[...] = first_pre
    act1_ref[...] = first_act
    cos1_ref[...] = first_cos
    second_pre = dot32(mw_ref[...], first_act, TN) + cols_ref[:, 2:3]
    second_act, second_cos = sine_cosine(second_pre * cols_ref[:, 3:4])
    pre2_ref[...] = second_pre
    cos2_ref[...] = second_cos
    for i, value in enumerate((second_act, second_act * feats_ref[0:1, :])):
        high, low = split_pair(value)
        act_ref[i * hidden : (i + 1) * hidden, :] = high
        act_ref[(i + 2) * hidden : (i + 3) * hidden, :] = low


def main_kernel(
    size,
    groups,
    filter_len,
    first,
    last,
    chunk,
    xk_ref,
    gk_ref,
    e1_ref,
    e2_ref,
    za_ref,
    zb_ref,
    s3_ref,
    fwd_ref,
    inv_ref,
    act_ref,
    head_ref,
    rates_ref,
    *rest,
):
    rest = list(rest)
    second_in = None if first else rest.pop(0)
    if last:
        net_in, rest = rest[:8], rest[8:]
        part_ref, net_ref, stage, sems, spec, prod, hold, delta, second_ref = rest
    else:
        part_ref, second_ref, stage, sems, spec, prod, hold, delta = rest
    seq = lax.axis_index("seq")
    par, odd = seq % 2, (seq // 2) % 2
    width = e1_ref.shape[1]
    hidden = head_ref.shape[0]
    mid = size // 2
    half = head_ref.shape[1] // 2
    here = pl.ds(pl.multiple_of(par * half + chunk * width, width), width)
    before, beyond = WINDOWED - 2 * par, BEYOND + 2 * par
    sources = [
        (xk_ref.at[:, here], (WINDOWED + 4) * (1 - par)),
        (gk_ref.at[:, here], (WINDOWED + 4) * par),
        (za_ref, beyond + odd * (before - beyond)),
        (zb_ref, before + odd * (beyond - before)),
        (e1_ref, WINDOWED + 6),
        (e2_ref, FIXED + 2),
        (s3_ref, WINDOWED + 2),
    ]
    copies = [
        pltpu.make_async_copy(source, stage.at[i], sems.at[i])
        for i, (source, _) in enumerate(sources)
    ]
    for copy in copies:
        copy.start()
    for n, (_, slot) in enumerate(sources):
        copies[n].wait()
        for i in range(2):
            block = stage[n, i * size : (i + 1) * size, :]
            both = dot16(fwd_ref[par], block)
            spec[slot + (i ^ par)] = both[: 2 * size] + both[2 * size :]

    lanes = 128
    rows = 16
    tiles = mid // rows

    def products(row, lane, sign):
        def load(slot):
            return (
                spec[slot, pl.ds(row, rows), pl.ds(lane, lanes)],
                spec[slot, pl.ds(row + size, rows), pl.ds(lane, lanes)],
            )

        acc_re = [None] * groups
        acc_im = [None] * groups

        def add(m, g, w):
            re = g[0] * w[0] + g[1] * w[1]
            im = g[0] * w[1] - g[1] * w[0]
            acc_re[m] = re if acc_re[m] is None else acc_re[m] + re
            acc_im[m] = im if acc_im[m] is None else acc_im[m] + im

        fixed = [load(FIXED + b) for b in range(4)]
        prev = None
        for j in range(8):
            now = load(WINDOWED + j)
            if prev is None:
                w = (now[1], -now[0]) if sign > 0 else (-now[1], now[0])
            elif sign > 0:
                w = (prev[0] + now[1], prev[1] - now[0])
            else:
                w = (prev[0] - now[1], prev[1] + now[0])
            for b, jj, m in block_pairs(groups):
                if jj == j:
                    add(m, fixed[b], w)
            if j == 3:
                near, far = load(BEYOND), load(BEYOND + 1)
                add(5, near, w)
                add(4, near, now)
                add(5, far, now)
            prev = now
        return acc_re, acc_im

    def body(it, carry):
        row = pl.multiple_of((it % tiles) * rows, rows)
        lane = pl.multiple_of((it // tiles) * lanes, lanes)
        even_re, even_im = products(row, lane, 1)
        for m in range(groups):
            hold[2 * m] = even_re[m]
            hold[2 * m + 1] = even_im[m]
        odd_re, odd_im = products(row + mid, lane, -1)
        for m in range(groups):
            re, im = hold[2 * m], hold[2 * m + 1]
            folded = (re + odd_re[m], im - odd_im[m], re - odd_re[m], im + odd_im[m])
            for part, value in enumerate(folded):
                high, low = split_pair(value)
                at = (pl.ds(row + part * mid, rows), pl.ds(lane, lanes))
                prod[2 * m, at[0], at[1]] = high
                prod[2 * m + 1, at[0], at[1]] = low
        return carry

    lax.fori_loop(0, tiles * (width // lanes), body, 0)

    rates = rates_ref[:, here]
    tap = lax.broadcasted_iota(jnp.int32, (size, width), 0)
    tap = jnp.where(tap < mid, 2 * tap, 2 * (tap - mid) + 1)
    inner = jnp.exp(-(tap.astype(jnp.float32) / filter_len) * rates)
    head = head_ref[:, here]
    head_high, head_low = split_pair(head)
    for m in range(groups):
        outer = jnp.exp(-(m * size / filter_len) * rates)
        for q in range(2):
            high = prod[2 * m, q * size : (q + 1) * size, :]
            low = prod[2 * m + 1, q * size : (q + 1) * size, :]
            both = dot16(inv_ref[q], high)
            grad = both[:mid] + both[mid:] + dot16(inv_ref[q, :mid, :], low)
            high, low = split_pair(grad * (inner[q * mid : (q + 1) * mid] * outer))
            at = m * size + q * mid
            delta[0, at : at + mid, :] = high
            delta[1, at : at + mid, :] = low
    stacked = dot16(act_ref[...], delta[0])
    total = (
        stacked[: 2 * hidden] + stacked[2 * hidden :] + dot16(act_ref[: 2 * hidden, :], delta[1])
    )
    stacked = dot16(jnp.concatenate([head_high, head_low], axis=0), delta[0], NT)
    second = stacked[:hidden] + stacked[hidden:] + dot16(head_high, delta[1], NT)
    second_ref[...] = second if first else second + second_in[...]

    part_ref[:hidden, :] = total[:hidden]
    part_ref[hidden:, :] = jnp.broadcast_to(
        -jnp.sum(total[hidden:] * head, axis=0, keepdims=True),
        (part_ref.shape[0] - hidden, width),
    )

    if last:
        mix, cols, feats, pre1, act1, cos1, pre2, cos2 = (r[...] for r in net_in)
        mix_freq, emb_freq = cols[:, 3:4], cols[:, 1:2]
        slope2 = second_ref[...] * cos2
        delta2 = slope2 * mix_freq
        slope1 = dot32(mix, delta2) * cos1
        delta1 = slope1 * emb_freq
        count = feats.shape[0]
        net_ref[:, :hidden] = dot32(delta2, act1, NT)
        net_ref[:, hidden : hidden + count] = dot32(delta1, feats, NT)
        for i, value in enumerate((delta1, slope1 * pre1, delta2, slope2 * pre2)):
            at = hidden + count + i
            net_ref[:, at : at + 1] = jnp.sum(value, axis=1, keepdims=True)
        at = hidden + count + 4
        net_ref[:, at:] = jnp.zeros((hidden, net_ref.shape[1] - at), jnp.float32)


def finish_kernel(count, net_ref, far_ref, *rest):
    ew_ref, eb_ref, ef_ref, mw_ref, mb_ref, mf_ref, head_ref, rates_ref = rest[-8:]
    parts = rest[:-8]
    par = lax.axis_index("seq") % 2
    turned = (net_ref[...] + far_ref[...]).T
    hidden = turned.shape[1]
    mw_ref[...] = turned[:hidden]
    ew_ref[...] = turned[hidden : hidden + count]
    for i, ref in enumerate((eb_ref, ef_ref, mb_ref, mf_ref)):
        ref[...] = turned[hidden + count + i : hidden + count + i + 1]
    width = parts[0].shape[1]
    half = head_ref.shape[1] // 2
    for i in range(len(parts) // 2):
        for which, ref in ((par, parts[2 * i]), (1 - par, parts[2 * i + 1])):
            at = pl.ds(pl.multiple_of(which * half + i * width, width), width)
            head_ref[:, at] = ref[:hidden, :]
            rates_ref[:, at] = ref[hidden : hidden + 1, :]


def after(value, *others):
    return lax.optimization_barrier((value, *others))[0]


def work(
    inputs,
    out_grad,
    embed_weight,
    embed_bias,
    embed_freq,
    mixer_weight,
    mixer_bias,
    mixer_freq,
    head_weight,
    decay_rates,
):
    block_len, chan_count = inputs.shape
    hidden = head_weight.shape[0]
    half = chan_count // 2
    size = block_len // 2
    filter_len = SPAN_PARTS * block_len
    groups = filter_len // size
    par = lax.axis_index("seq") % 2
    count = lax.axis_size("seq")
    width = min(256, half)
    chunks = range(half // width)

    def part_of(value, which, chunk, span):
        start = which * half + chunk * span
        return lax.dynamic_slice_in_dim(value, start, span, axis=1)

    def gives(inputs, out_grad, chunk):
        x_give = part_of(inputs, 1 - par, chunk, width)
        g_give = part_of(out_grad, 1 - par, chunk, width)
        return jnp.where(par == 0, g_give, x_give), jnp.where(par == 0, x_give, g_give)

    odd = (lax.axis_index("seq") // 2) % 2
    ahead = [(i, i + 2) for i in range(0, count - 2, 2)]
    back = [(i, i - 2) for i in range(3, count, 2)]
    upper = [i for i in range(count - 2) if (i // 2) % 2 == 1]
    middle = [(i, i + 2) for i in upper] + [(i + 2, i) for i in upper]

    def halos(x_all, g_all, chunk):
        x_keep = part_of(x_all, par, chunk, width)
        g_keep = part_of(g_all, par, chunk, width)
        return jnp.where(odd == 0, x_keep, g_keep), jnp.where(odd == 0, g_keep, x_keep)

    e1, e2, s3, za, zb = [], [], [], [], []
    own_in, own_grad = inputs, out_grad
    for c in chunks:
        one, _ = gives(own_in, own_grad, c)
        e1.append(swapped(one, "seq", 1))
        own_in, own_grad, _ = lax.optimization_barrier((own_in, own_grad, one))
    for c in chunks:
        up, down = halos(own_in, own_grad, c)
        za.append(swapped(up, "seq", 2))
        zb.append(lax.ppermute(down, "seq", middle))
        own_in, own_grad, _, _ = lax.optimization_barrier((own_in, own_grad, up, down))
    for c in chunks:
        _, two = gives(own_in, own_grad, c)
        s3.append(lax.ppermute(e1[c], "seq", ahead + back))
        e2.append(swapped(after(two, e1[c]), "seq", 1))

    features = jnp.asarray(tap_features(filter_len, size, BANDS))
    feats = features.shape[0]
    taps = jax.ShapeDtypeStruct((hidden, filter_len), jnp.float32)
    wide = jax.ShapeDtypeStruct((4 * hidden, filter_len), jnp.bfloat16)
    vmem = pl.BlockSpec(memory_space=pltpu.VMEM)
    made = pl.pallas_call(
        prep_kernel,
        in_specs=[vmem] * 7,
        out_specs=[vmem] * 7,
        out_shape=[wide] + [taps] * 5 + [jax.ShapeDtypeStruct((hidden, 8), jnp.float32)],
        compiler_params=pltpu.CompilerParams(vmem_limit_bytes=16 * 2**20),
        name="prep",
    )(
        after(embed_weight, e1[0]),
        embed_bias[None, :],
        embed_freq[None, :],
        mixer_weight,
        mixer_bias[None, :],
        mixer_freq[None, :],
        features,
    )
    act, first_pre, first_act, first_cos, second_pre, second_cos, cols = made

    (fwd_high, fwd_low), (inv_high, inv_low) = transforms(size)
    forward = np.concatenate([fwd_high, fwd_low], axis=0)
    mirrored = forward * np.where(np.arange(4 * size) // size % 2, -1, 1)[:, None].astype(forward.dtype)
    forward = jnp.asarray(np.stack([forward, mirrored]))
    mid = size // 2
    inverse = jnp.asarray(
        np.stack(
            [
                np.concatenate([inv_high[q * mid : (q + 1) * mid], inv_low[q * mid : (q + 1) * mid]])
                for q in range(2)
            ]
        )
    )

    parts = []
    second_grad = None
    late_in, late_grad, _ = lax.optimization_barrier((inputs, out_grad, e1[0]))
    for c in chunks:
        first, last = c == 0, c == chunks[-1]
        operands = [
            late_in,
            late_grad,
            e1[c],
            e2[c],
            za[c],
            zb[c],
            s3[c],
            forward,
            inverse,
            act,
            head_weight,
            decay_rates[None, :],
        ]
        if not first:
            operands.append(second_grad)
        part_shape = jax.ShapeDtypeStruct((hidden + 8, width), jnp.float32)
        second_shape = jax.ShapeDtypeStruct((hidden, filter_len), jnp.float32)
        scratch = [
            pltpu.VMEM((7, block_len, width), jnp.bfloat16),
            pltpu.SemaphoreType.DMA((7,)),
            pltpu.VMEM((14, 2 * size, width), jnp.float32),
            pltpu.VMEM((2 * groups, 2 * size, width), jnp.bfloat16),
            pltpu.VMEM((2 * groups, 16, 128), jnp.float32),
            pltpu.VMEM((2, filter_len, width), jnp.bfloat16),
        ]
        if last:
            operands += [
                mixer_weight,
                cols,
                features,
                first_pre,
                first_act,
                first_cos,
                second_pre,
                second_cos,
            ]
            out_shape = [part_shape, jax.ShapeDtypeStruct((hidden, 2 * hidden), jnp.float32)]
            scratch.append(pltpu.VMEM((hidden, filter_len), jnp.float32))
        else:
            out_shape = [part_shape, second_shape]
        part, out = pl.pallas_call(
            functools.partial(main_kernel, size, groups, filter_len, first, last, c),
            in_specs=[pl.BlockSpec(memory_space=pltpu.HBM)] * 7
            + [pl.BlockSpec(memory_space=pltpu.VMEM)] * (len(operands) - 7),
            out_specs=[pl.BlockSpec(memory_space=pltpu.VMEM)] * 2,
            out_shape=out_shape,
            scratch_shapes=scratch,
            compiler_params=pltpu.CompilerParams(vmem_limit_bytes=40 * 2**20),
            cost_estimate=pl.CostEstimate(
                flops=4 * 10**9, bytes_accessed=8 * 2**20, transcendentals=0
            ),
            name="filter_grad",
        )(*operands)
        parts.append(part)
        if last:
            net = out
        else:
            second_grad = out

    far_bits = bits_of("seq", 2)
    steps = [("chan", b) for b in bits_of("chan")] + [("seq", b) for b in far_bits]
    for axis, bit in steps:
        net = net + swapped(net, axis, bit)
    far = swapped(net, "seq", 1)
    both = []
    for p in parts:
        for bit in far_bits:
            p = p + swapped(p, "seq", bit)
        both += [p, swapped(p, "seq", 1)]

    row = jax.ShapeDtypeStruct((1, hidden), jnp.float32)
    outs = pl.pallas_call(
        functools.partial(finish_kernel, feats),
        in_specs=[pl.BlockSpec(memory_space=pltpu.VMEM)] * (2 + len(both)),
        out_specs=[pl.BlockSpec(memory_space=pltpu.VMEM)] * 8,
        out_shape=[
            jax.ShapeDtypeStruct((feats, hidden), jnp.float32),
            row,
            row,
            jax.ShapeDtypeStruct((hidden, hidden), jnp.float32),
            row,
            row,
            jax.ShapeDtypeStruct((hidden, chan_count), jnp.float32),
            jax.ShapeDtypeStruct((1, chan_count), jnp.float32),
        ],
        compiler_params=pltpu.CompilerParams(vmem_limit_bytes=8 * 2**20),
        name="finish",
    )(net, far, *both)
    return tuple(o[0] if o.shape[0] == 1 else o for o in outs)


def solution(mesh):
    in_specs = (
        P("seq", "chan"),
        P("seq", "chan"),
        P(),
        P(),
        P(),
        P(),
        P(),
        P(),
        P(None, "chan"),
        P("chan"),
    )
    out_specs = (P(), P(), P(), P(), P(), P(), P(None, "chan"), P("chan"))
    return jax.shard_map(work, mesh=mesh, in_specs=in_specs, out_specs=out_specs, check_vma=False)
```

```python
import functools
import math

import jax
import jax.numpy as jnp
import numpy as np
from jax import lax
from jax.experimental import pallas as pl
from jax.experimental.pallas import tpu as pltpu
from jax.sharding import PartitionSpec as P


BANDS = 8
SPAN_PARTS = 3


def swapped(value, axis, bit):
    return lax.ppermute(value, axis, [(i, i ^ bit) for i in range(lax.axis_size(axis))])


def bits_of(axis, first=1):
    count = lax.axis_size(axis)
    assert count & (count - 1) == 0
    return [1 << i for i in range(count.bit_length() - 1) if (1 << i) >= first]


def split_const(matrix):
    high = matrix.astype(np.float32).astype(jnp.bfloat16)
    low = (matrix - high.astype(np.float64)).astype(np.float32).astype(jnp.bfloat16)
    return high, low


@functools.cache
def transforms(size):
    freqs = np.arange(0, size, 2)
    freqs = np.concatenate([freqs, size - 1 - freqs])
    omega = np.pi * (2 * freqs + 1) / (2 * size)
    steps = np.arange(size)
    forward = np.concatenate(
        [np.cos(omega[:, None] * steps), -np.sin(omega[:, None] * steps)], axis=0
    )
    omega = omega[: size // 2]
    dist = size - tap_order(size)
    inverse = (
        np.concatenate(
            [np.cos(dist[:, None] * omega), -np.sin(dist[:, None] * omega)], axis=1
        )
        / size
    )
    return split_const(forward), split_const(inverse)


def tap_order(size):
    return np.concatenate([np.arange(0, size, 2), np.arange(1, size, 2)])


def split_pair(value):
    high = value.astype(jnp.bfloat16)
    return high, (value - high.astype(jnp.float32)).astype(jnp.bfloat16)


@functools.cache
def tap_features(filter_len, size, band_count):
    tap = np.concatenate([m * size + tap_order(size) for m in range(filter_len // size)])
    scaled = tap.astype(np.float32) / np.float32(filter_len)
    rates = [max(1, filter_len // 4 // 2 ** (band_count - i)) for i in range(1, band_count + 1)]
    cycles = np.array(rates)[:, None] * tap[None, :] % filter_len
    angle = cycles.astype(np.float32) * np.float32(2.0 * math.pi / filter_len)
    angle = angle.astype(np.float64)
    return np.concatenate([scaled[None, :], np.cos(angle), np.sin(angle)], axis=0).astype(
        np.float32
    )


def dot16(left, right, dims=(((1,), (0,)), ((), ()))):
    return lax.dot_general(left, right, dims, preferred_element_type=jnp.float32)


def dot32(left, right, dims=(((1,), (0,)), ((), ()))):
    left_high, left_low = split_pair(left)
    right_high, right_low = split_pair(right)
    return (
        dot16(left_high, right_high, dims)
        + dot16(left_high, right_low, dims)
        + dot16(left_low, right_high, dims)
    )


NT = (((1,), (1,)), ((), ()))
FIXED, BEYOND, WINDOWED = 0, 4, 6


def block_pairs(groups):
    return [(b, j, b + 4 - j) for j in range(8) for b in range(4) if 0 <= b + 4 - j < groups]


TN = (((0,), (0,)), ((), ()))
SIN_TERMS = [(-1.0) ** i / math.factorial(2 * i + 1) for i in range(6)]
COS_TERMS = [(-1.0) ** i / math.factorial(2 * i) for i in range(7)]


def sine_cosine(angle):
    turns = jnp.floor(angle * (1.0 / math.pi) + 0.5)
    rest = angle - turns * 3.140625
    rest = rest - turns * 9.67502593994140625e-4
    rest = rest - turns * 1.509957990978376432e-7
    sign = 1.0 - 4.0 * (0.5 * turns - jnp.floor(0.5 * turns))
    square = rest * rest
    sine = SIN_TERMS[-1]
    for term in SIN_TERMS[-2::-1]:
        sine = sine * square + term
    cosine = COS_TERMS[-1]
    for term in COS_TERMS[-2::-1]:
        cosine = cosine * square + term
    return sine * (rest * sign), cosine * sign


def prep_kernel(
    ew_ref,
    eb_ref,
    ef_ref,
    mw_ref,
    mb_ref,
    mf_ref,
    feats_ref,
    act_ref,
    pre1_ref,
    act1_ref,
    cos1_ref,
    pre2_ref,
    cos2_ref,
    cols_ref,
):
    hidden = mw_ref.shape[0]
    vectors = jnp.concatenate(
        [eb_ref[...], ef_ref[...], mb_ref[...], mf_ref[...]] * 2, axis=0
    )
    vectors = jnp.concatenate([vectors, jnp.zeros_like(vectors)], axis=1).T
    cols_ref[...] = vectors[:hidden]
    first_pre = dot32(ew_ref[...], feats_ref[...], TN) + cols_ref[:, 0:1]
    first_act, first_cos = sine_cosine(first_pre * cols_ref[:, 1:2])
    pre1_ref[...] = first_pre
    act1_ref[...] = first_act
    cos1_ref[...] = first_cos
    second_pre = dot32(mw_ref[...], first_act, TN) + cols_ref[:, 2:3]
    second_act, second_cos = sine_cosine(second_pre * cols_ref[:, 3:4])
    pre2_ref[...] = second_pre
    cos2_ref[...] = second_cos
    for i, value in enumerate((second_act, second_act * feats_ref[0:1, :])):
        high, low = split_pair(value)
        act_ref[i * hidden : (i + 1) * hidden, :] = high
        act_ref[(i + 2) * hidden : (i + 3) * hidden, :] = low


def main_kernel(
    size,
    groups,
    filter_len,
    first,
    last,
    chunk,
    xk_ref,
    gk_ref,
    e1_ref,
    e2_ref,
    za_ref,
    zb_ref,
    s3_ref,
    fwd_ref,
    inv_ref,
    act_ref,
    head_ref,
    rates_ref,
    *rest,
):
    rest = list(rest)
    second_in = None if first else rest.pop(0)
    if last:
        net_in, rest = rest[:8], rest[8:]
        part_ref, net_ref, stage, sems, spec, prod, hold, delta, second_ref = rest
    else:
        part_ref, second_ref, stage, sems, spec, prod, hold, delta = rest
    seq = lax.axis_index("seq")
    par, odd = seq % 2, (seq // 2) % 2
    width = e1_ref.shape[1]
    hidden = head_ref.shape[0]
    mid = size // 2
    half = head_ref.shape[1] // 2
    here = pl.ds(pl.multiple_of(par * half + chunk * width, width), width)
    before, beyond = WINDOWED - 2 * par, BEYOND + 2 * par
    sources = [
        (xk_ref.at[:, here], (WINDOWED + 4) * (1 - par)),
        (gk_ref.at[:, here], (WINDOWED + 4) * par),
        (za_ref, beyond + odd * (before - beyond)),
        (zb_ref, before + odd * (beyond - before)),
        (e1_ref, WINDOWED + 6),
        (e2_ref, FIXED + 2),
        (s3_ref, WINDOWED + 2),
    ]
    copies = [
        pltpu.make_async_copy(source, stage.at[i], sems.at[i])
        for i, (source, _) in enumerate(sources)
    ]
    for copy in copies:
        copy.start()
    for n, (_, slot) in enumerate(sources):
        copies[n].wait()
        for i in range(2):
            block = stage[n, i * size : (i + 1) * size, :]
            both = dot16(fwd_ref[par], block)
            spec[slot + (i ^ par)] = both[: 2 * size] + both[2 * size :]

    lanes = 128
    rows = 16
    tiles = mid // rows

    def products(row, lane, sign):
        def load(slot):
            return (
                spec[slot, pl.ds(row, rows), pl.ds(lane, lanes)],
                spec[slot, pl.ds(row + size, rows), pl.ds(lane, lanes)],
            )

        acc_re = [None] * groups
        acc_im = [None] * groups

        def add(m, g, w):
            re = g[0] * w[0] + g[1] * w[1]
            im = g[0] * w[1] - g[1] * w[0]
            acc_re[m] = re if acc_re[m] is None else acc_re[m] + re
            acc_im[m] = im if acc_im[m] is None else acc_im[m] + im

        fixed = [load(FIXED + b) for b in range(4)]
        prev = None
        for j in range(8):
            now = load(WINDOWED + j)
            if prev is None:
                w = (now[1], -now[0]) if sign > 0 else (-now[1], now[0])
            elif sign > 0:
                w = (prev[0] + now[1], prev[1] - now[0])
            else:
                w = (prev[0] - now[1], prev[1] + now[0])
            for b, jj, m in block_pairs(groups):
                if jj == j:
                    add(m, fixed[b], w)
            if j == 3:
                near, far = load(BEYOND), load(BEYOND + 1)
                add(5, near, w)
                add(4, near, now)
                add(5, far, now)
            prev = now
        return acc_re, acc_im

    def body(it, carry):
        row = pl.multiple_of((it % tiles) * rows, rows)
        lane = pl.multiple_of((it // tiles) * lanes, lanes)
        even_re, even_im = products(row, lane, 1)
        for m in range(groups):
            hold[2 * m] = even_re[m]
            hold[2 * m + 1] = even_im[m]
        odd_re, odd_im = products(row + mid, lane, -1)
        for m in range(groups):
            re, im = hold[2 * m], hold[2 * m + 1]
            folded = (re + odd_re[m], im - odd_im[m], re - odd_re[m], im + odd_im[m])
            for part, value in enumerate(folded):
                high, low = split_pair(value)
                at = (pl.ds(row + part * mid, rows), pl.ds(lane, lanes))
                prod[2 * m, at[0], at[1]] = high
                prod[2 * m + 1, at[0], at[1]] = low
        return carry

    lax.fori_loop(0, tiles * (width // lanes), body, 0)

    rates = rates_ref[:, here]
    tap = lax.broadcasted_iota(jnp.int32, (size, width), 0)
    tap = jnp.where(tap < mid, 2 * tap, 2 * (tap - mid) + 1)
    inner = jnp.exp(-(tap.astype(jnp.float32) / filter_len) * rates)
    head = head_ref[:, here]
    head_high, head_low = split_pair(head)
    for m in range(groups):
        outer = jnp.exp(-(m * size / filter_len) * rates)
        for q in range(2):
            high = prod[2 * m, q * size : (q + 1) * size, :]
            low = prod[2 * m + 1, q * size : (q + 1) * size, :]
            both = dot16(inv_ref[q], high)
            grad = both[:mid] + both[mid:] + dot16(inv_ref[q, :mid, :], low)
            high, low = split_pair(grad * (inner[q * mid : (q + 1) * mid] * outer))
            at = m * size + q * mid
            delta[0, at : at + mid, :] = high
            delta[1, at : at + mid, :] = low
    stacked = dot16(act_ref[...], delta[0])
    total = (
        stacked[: 2 * hidden] + stacked[2 * hidden :] + dot16(act_ref[: 2 * hidden, :], delta[1])
    )
    stacked = dot16(jnp.concatenate([head_high, head_low], axis=0), delta[0], NT)
    second = stacked[:hidden] + stacked[hidden:] + dot16(head_high, delta[1], NT)
    second_ref[...] = second if first else second + second_in[...]

    part_ref[:hidden, :] = total[:hidden]
    part_ref[hidden:, :] = jnp.broadcast_to(
        -jnp.sum(total[hidden:] * head, axis=0, keepdims=True),
        (part_ref.shape[0] - hidden, width),
    )

    if last:
        mix, cols, feats, pre1, act1, cos1, pre2, cos2 = (r[...] for r in net_in)
        mix_freq, emb_freq = cols[:, 3:4], cols[:, 1:2]
        slope2 = second_ref[...] * cos2
        delta2 = slope2 * mix_freq
        slope1 = dot32(mix, delta2) * cos1
        delta1 = slope1 * emb_freq
        count = feats.shape[0]
        net_ref[:, :hidden] = dot32(delta2, act1, NT)
        net_ref[:, hidden : hidden + count] = dot32(delta1, feats, NT)
        for i, value in enumerate((delta1, slope1 * pre1, delta2, slope2 * pre2)):
            at = hidden + count + i
            net_ref[:, at : at + 1] = jnp.sum(value, axis=1, keepdims=True)
        at = hidden + count + 4
        net_ref[:, at:] = jnp.zeros((hidden, net_ref.shape[1] - at), jnp.float32)


def finish_kernel(count, net_ref, far_ref, *rest):
    ew_ref, eb_ref, ef_ref, mw_ref, mb_ref, mf_ref, head_ref, rates_ref = rest[-8:]
    parts = rest[:-8]
    par = lax.axis_index("seq") % 2
    turned = (net_ref[...] + far_ref[...]).T
    hidden = turned.shape[1]
    mw_ref[...] = turned[:hidden]
    ew_ref[...] = turned[hidden : hidden + count]
    for i, ref in enumerate((eb_ref, ef_ref, mb_ref, mf_ref)):
        ref[...] = turned[hidden + count + i : hidden + count + i + 1]
    width = parts[0].shape[1]
    half = head_ref.shape[1] // 2
    for i in range(len(parts) // 2):
        for which, ref in ((par, parts[2 * i]), (1 - par, parts[2 * i + 1])):
            at = pl.ds(pl.multiple_of(which * half + i * width, width), width)
            head_ref[:, at] = ref[:hidden, :]
            rates_ref[:, at] = ref[hidden : hidden + 1, :]


def after(value, *others):
    return lax.optimization_barrier((value, *others))[0]


def work(
    inputs,
    out_grad,
    embed_weight,
    embed_bias,
    embed_freq,
    mixer_weight,
    mixer_bias,
    mixer_freq,
    head_weight,
    decay_rates,
):
    block_len, chan_count = inputs.shape
    hidden = head_weight.shape[0]
    half = chan_count // 2
    size = block_len // 2
    filter_len = SPAN_PARTS * block_len
    groups = filter_len // size
    par = lax.axis_index("seq") % 2
    count = lax.axis_size("seq")
    width = min(256, half)
    chunks = range(half // width)

    def columns(value, which, chunk):
        start = which * half + chunk * width
        return value[:, start : start + width]

    def gives(x_all, g_all, chunk):
        one = jnp.where(par == 0, columns(g_all, 1, chunk), columns(x_all, 0, chunk))
        two = jnp.where(par == 0, columns(x_all, 1, chunk), columns(g_all, 0, chunk))
        return one, two

    odd = (lax.axis_index("seq") // 2) % 2
    ahead = [(i, i + 2) for i in range(0, count - 2, 2)]
    back = [(i, i - 2) for i in range(3, count, 2)]
    upper = [i for i in range(count - 2) if (i // 2) % 2 == 1]
    middle = [(i, i + 2) for i in upper] + [(i + 2, i) for i in upper]

    def halos(x_all, g_all, chunk):
        x_keep = jnp.where(par == 0, columns(x_all, 0, chunk), columns(x_all, 1, chunk))
        g_keep = jnp.where(par == 0, columns(g_all, 0, chunk), columns(g_all, 1, chunk))
        return jnp.where(odd == 0, x_keep, g_keep), jnp.where(odd == 0, g_keep, x_keep)

    e1, e2, s3, za, zb = [], [], [], [], []
    own_in, own_grad = inputs, out_grad
    for c in chunks:
        one, _ = gives(own_in, own_grad, c)
        e1.append(swapped(one, "seq", 1))
        own_in, own_grad, _ = lax.optimization_barrier((own_in, own_grad, one))
    for c in chunks:
        up, down = halos(own_in, own_grad, c)
        za.append(swapped(up, "seq", 2))
        zb.append(lax.ppermute(down, "seq", middle))
        own_in, own_grad, _, _ = lax.optimization_barrier((own_in, own_grad, up, down))
    for c in chunks:
        _, two = gives(own_in, own_grad, c)
        s3.append(lax.ppermute(e1[c], "seq", ahead + back))
        e2.append(swapped(after(two, e1[c]), "seq", 1))

    features = jnp.asarray(tap_features(filter_len, size, BANDS))
    feats = features.shape[0]
    taps = jax.ShapeDtypeStruct((hidden, filter_len), jnp.float32)
    wide = jax.ShapeDtypeStruct((4 * hidden, filter_len), jnp.bfloat16)
    vmem = pl.BlockSpec(memory_space=pltpu.VMEM)
    made = pl.pallas_call(
        prep_kernel,
        in_specs=[vmem] * 7,
        out_specs=[vmem] * 7,
        out_shape=[wide] + [taps] * 5 + [jax.ShapeDtypeStruct((hidden, 8), jnp.float32)],
        compiler_params=pltpu.CompilerParams(vmem_limit_bytes=16 * 2**20),
        name="prep",
    )(
        after(embed_weight, e1[0]),
        embed_bias[None, :],
        embed_freq[None, :],
        mixer_weight,
        mixer_bias[None, :],
        mixer_freq[None, :],
        features,
    )
    act, first_pre, first_act, first_cos, second_pre, second_cos, cols = made

    (fwd_high, fwd_low), (inv_high, inv_low) = transforms(size)
    forward = np.concatenate([fwd_high, fwd_low], axis=0)
    mirrored = forward * np.where(np.arange(4 * size) // size % 2, -1, 1)[:, None].astype(forward.dtype)
    forward = jnp.asarray(np.stack([forward, mirrored]))
    mid = size // 2
    inverse = jnp.asarray(
        np.stack(
            [
                np.concatenate([inv_high[q * mid : (q + 1) * mid], inv_low[q * mid : (q + 1) * mid]])
                for q in range(2)
            ]
        )
    )

    parts = []
    second_grad = None
    late_in, late_grad, _ = lax.optimization_barrier((inputs, out_grad, e1[0]))
    for c in chunks:
        first, last = c == 0, c == chunks[-1]
        operands = [
            late_in,
            late_grad,
            e1[c],
            e2[c],
            za[c],
            zb[c],
            s3[c],
            forward,
            inverse,
            act,
            head_weight,
            decay_rates[None, :],
        ]
        if not first:
            operands.append(second_grad)
        part_shape = jax.ShapeDtypeStruct((hidden + 8, width), jnp.float32)
        second_shape = jax.ShapeDtypeStruct((hidden, filter_len), jnp.float32)
        scratch = [
            pltpu.VMEM((7, block_len, width), jnp.bfloat16),
            pltpu.SemaphoreType.DMA((7,)),
            pltpu.VMEM((14, 2 * size, width), jnp.float32),
            pltpu.VMEM((2 * groups, 2 * size, width), jnp.bfloat16),
            pltpu.VMEM((2 * groups, 16, 128), jnp.float32),
            pltpu.VMEM((2, filter_len, width), jnp.bfloat16),
        ]
        if last:
            operands += [
                mixer_weight,
                cols,
                features,
                first_pre,
                first_act,
                first_cos,
                second_pre,
                second_cos,
            ]
            out_shape = [part_shape, jax.ShapeDtypeStruct((hidden, 2 * hidden), jnp.float32)]
            scratch.append(pltpu.VMEM((hidden, filter_len), jnp.float32))
        else:
            out_shape = [part_shape, second_shape]
        part, out = pl.pallas_call(
            functools.partial(main_kernel, size, groups, filter_len, first, last, c),
            in_specs=[pl.BlockSpec(memory_space=pltpu.HBM)] * 7
            + [pl.BlockSpec(memory_space=pltpu.VMEM)] * (len(operands) - 7),
            out_specs=[pl.BlockSpec(memory_space=pltpu.VMEM)] * 2,
            out_shape=out_shape,
            scratch_shapes=scratch,
            compiler_params=pltpu.CompilerParams(vmem_limit_bytes=40 * 2**20),
            cost_estimate=pl.CostEstimate(
                flops=4 * 10**9, bytes_accessed=8 * 2**20, transcendentals=0
            ),
            name="filter_grad",
        )(*operands)
        parts.append(part)
        if last:
            net = out
        else:
            second_grad = out

    far_bits = bits_of("seq", 2)
    steps = [("chan", b) for b in bits_of("chan")] + [("seq", b) for b in far_bits]
    for axis, bit in steps:
        net = net + swapped(net, axis, bit)
    far = swapped(net, "seq", 1)
    both = []
    for p in parts:
        for bit in far_bits:
            p = p + swapped(p, "seq", bit)
        both += [p, swapped(p, "seq", 1)]

    row = jax.ShapeDtypeStruct((1, hidden), jnp.float32)
    outs = pl.pallas_call(
        functools.partial(finish_kernel, feats),
        in_specs=[pl.BlockSpec(memory_space=pltpu.VMEM)] * (2 + len(both)),
        out_specs=[pl.BlockSpec(memory_space=pltpu.VMEM)] * 8,
        out_shape=[
            jax.ShapeDtypeStruct((feats, hidden), jnp.float32),
            row,
            row,
            jax.ShapeDtypeStruct((hidden, hidden), jnp.float32),
            row,
            row,
            jax.ShapeDtypeStruct((hidden, chan_count), jnp.float32),
            jax.ShapeDtypeStruct((1, chan_count), jnp.float32),
        ],
        compiler_params=pltpu.CompilerParams(vmem_limit_bytes=8 * 2**20),
        name="finish",
    )(net, far, *both)
    return tuple(o[0] if o.shape[0] == 1 else o for o in outs)


def solution(mesh):
    in_specs = (
        P("seq", "chan"),
        P("seq", "chan"),
        P(),
        P(),
        P(),
        P(),
        P(),
        P(),
        P(None, "chan"),
        P("chan"),
    )
    out_specs = (P(), P(), P(), P(), P(), P(), P(None, "chan"), P("chan"))
    return jax.shard_map(work, mesh=mesh, in_specs=in_specs, out_specs=out_specs, check_vma=False)
```

```python
import functools
import math

import jax
import jax.numpy as jnp
import numpy as np
from jax import lax
from jax.experimental import pallas as pl
from jax.experimental.pallas import tpu as pltpu
from jax.sharding import PartitionSpec as P


BANDS = 8
SPAN_PARTS = 3


def swapped(value, axis, bit):
    return lax.ppermute(value, axis, [(i, i ^ bit) for i in range(lax.axis_size(axis))])


def bits_of(axis, first=1):
    count = lax.axis_size(axis)
    assert count & (count - 1) == 0
    return [1 << i for i in range(count.bit_length() - 1) if (1 << i) >= first]


def split_const(matrix):
    high = matrix.astype(np.float32).astype(jnp.bfloat16)
    low = (matrix - high.astype(np.float64)).astype(np.float32).astype(jnp.bfloat16)
    return high, low


@functools.cache
def transforms(size):
    freqs = np.arange(0, size, 2)
    freqs = np.concatenate([freqs, size - 1 - freqs])
    omega = np.pi * (2 * freqs + 1) / (2 * size)
    steps = np.arange(size)
    forward = np.concatenate(
        [np.cos(omega[:, None] * steps), -np.sin(omega[:, None] * steps)], axis=0
    )
    omega = omega[: size // 2]
    dist = size - tap_order(size)
    inverse = (
        np.concatenate(
            [np.cos(dist[:, None] * omega), -np.sin(dist[:, None] * omega)], axis=1
        )
        / size
    )
    return split_const(forward), split_const(inverse)


def tap_order(size):
    return np.concatenate([np.arange(0, size, 2), np.arange(1, size, 2)])


def split_pair(value):
    high = value.astype(jnp.bfloat16)
    return high, (value - high.astype(jnp.float32)).astype(jnp.bfloat16)


@functools.cache
def tap_features(filter_len, size, band_count):
    tap = np.concatenate([m * size + tap_order(size) for m in range(filter_len // size)])
    scaled = tap.astype(np.float32) / np.float32(filter_len)
    rates = [max(1, filter_len // 4 // 2 ** (band_count - i)) for i in range(1, band_count + 1)]
    cycles = np.array(rates)[:, None] * tap[None, :] % filter_len
    angle = cycles.astype(np.float32) * np.float32(2.0 * math.pi / filter_len)
    angle = angle.astype(np.float64)
    return np.concatenate([scaled[None, :], np.cos(angle), np.sin(angle)], axis=0).astype(
        np.float32
    )


def dot16(left, right, dims=(((1,), (0,)), ((), ()))):
    return lax.dot_general(left, right, dims, preferred_element_type=jnp.float32)


def dot32(left, right, dims=(((1,), (0,)), ((), ()))):
    left_high, left_low = split_pair(left)
    right_high, right_low = split_pair(right)
    return (
        dot16(left_high, right_high, dims)
        + dot16(left_high, right_low, dims)
        + dot16(left_low, right_high, dims)
    )


NT = (((1,), (1,)), ((), ()))
FIXED, BEYOND, WINDOWED = 0, 4, 6


def block_pairs(groups):
    return [(b, j, b + 4 - j) for j in range(8) for b in range(4) if 0 <= b + 4 - j < groups]


TN = (((0,), (0,)), ((), ()))
SIN_TERMS = [(-1.0) ** i / math.factorial(2 * i + 1) for i in range(6)]
COS_TERMS = [(-1.0) ** i / math.factorial(2 * i) for i in range(7)]


def sine_cosine(angle):
    turns = jnp.floor(angle * (1.0 / math.pi) + 0.5)
    rest = angle - turns * 3.140625
    rest = rest - turns * 9.67502593994140625e-4
    rest = rest - turns * 1.509957990978376432e-7
    sign = 1.0 - 4.0 * (0.5 * turns - jnp.floor(0.5 * turns))
    square = rest * rest
    sine = SIN_TERMS[-1]
    for term in SIN_TERMS[-2::-1]:
        sine = sine * square + term
    cosine = COS_TERMS[-1]
    for term in COS_TERMS[-2::-1]:
        cosine = cosine * square + term
    return sine * (rest * sign), cosine * sign


def prep_kernel(
    ew_ref,
    eb_ref,
    ef_ref,
    mw_ref,
    mb_ref,
    mf_ref,
    feats_ref,
    act_ref,
    pre1_ref,
    act1_ref,
    cos1_ref,
    pre2_ref,
    cos2_ref,
    cols_ref,
):
    hidden = mw_ref.shape[0]
    vectors = jnp.concatenate(
        [eb_ref[...], ef_ref[...], mb_ref[...], mf_ref[...]] * 2, axis=0
    )
    vectors = jnp.concatenate([vectors, jnp.zeros_like(vectors)], axis=1).T
    cols_ref[...] = vectors[:hidden]
    first_pre = dot32(ew_ref[...], feats_ref[...], TN) + cols_ref[:, 0:1]
    first_act, first_cos = sine_cosine(first_pre * cols_ref[:, 1:2])
    pre1_ref[...] = first_pre
    act1_ref[...] = first_act
    cos1_ref[...] = first_cos
    second_pre = dot32(mw_ref[...], first_act, TN) + cols_ref[:, 2:3]
    second_act, second_cos = sine_cosine(second_pre * cols_ref[:, 3:4])
    pre2_ref[...] = second_pre
    cos2_ref[...] = second_cos
    for i, value in enumerate((second_act, second_act * feats_ref[0:1, :])):
        high, low = split_pair(value)
        act_ref[i * hidden : (i + 1) * hidden, :] = high
        act_ref[(i + 2) * hidden : (i + 3) * hidden, :] = low


def main_kernel(
    size,
    groups,
    filter_len,
    first,
    last,
    chunk,
    xk_ref,
    gk_ref,
    e1_ref,
    e2_ref,
    za_ref,
    zb_ref,
    s3_ref,
    fwd_ref,
    inv_ref,
    act_ref,
    head_ref,
    rates_ref,
    *rest,
):
    rest = list(rest)
    second_in = None if first else rest.pop(0)
    if last:
        net_in, rest = rest[:8], rest[8:]
        part_ref, net_ref, stage, sems, spec, prod, hold, delta, second_ref = rest
    else:
        part_ref, second_ref, stage, sems, spec, prod, hold, delta = rest
    seq = lax.axis_index("seq")
    par, odd = seq % 2, (seq // 2) % 2
    width = e1_ref.shape[1]
    hidden = head_ref.shape[0]
    mid = size // 2
    half = head_ref.shape[1] // 2
    here = pl.ds(pl.multiple_of(par * half + chunk * width, width), width)
    before, beyond = WINDOWED - 2 * par, BEYOND + 2 * par
    sources = [
        (xk_ref.at[:, here], (WINDOWED + 4) * (1 - par)),
        (gk_ref.at[:, here], (WINDOWED + 4) * par),
        (za_ref, beyond + odd * (before - beyond)),
        (zb_ref, before + odd * (beyond - before)),
        (e1_ref, WINDOWED + 6),
        (e2_ref, FIXED + 2),
        (s3_ref, WINDOWED + 2),
    ]
    copies = [
        pltpu.make_async_copy(source, stage.at[i], sems.at[i])
        for i, (source, _) in enumerate(sources[:2])
    ]
    for copy in copies:
        copy.start()
    for n, (ref, slot) in enumerate(sources[2:] + sources[:2]):
        if n >= 5:
            copies[n - 5].wait()
            ref = stage.at[n - 5]
        for i in range(2):
            block = ref[i * size : (i + 1) * size, :]
            both = dot16(fwd_ref[par], block)
            spec[slot + (i ^ par)] = both[: 2 * size] + both[2 * size :]

    lanes = 128
    rows = 16
    tiles = mid // rows

    def products(row, lane, sign):
        def load(slot):
            return (
                spec[slot, pl.ds(row, rows), pl.ds(lane, lanes)],
                spec[slot, pl.ds(row + size, rows), pl.ds(lane, lanes)],
            )

        acc_re = [None] * groups
        acc_im = [None] * groups

        def add(m, g, w):
            re = g[0] * w[0] + g[1] * w[1]
            im = g[0] * w[1] - g[1] * w[0]
            acc_re[m] = re if acc_re[m] is None else acc_re[m] + re
            acc_im[m] = im if acc_im[m] is None else acc_im[m] + im

        fixed = [load(FIXED + b) for b in range(4)]
        prev = None
        for j in range(8):
            now = load(WINDOWED + j)
            if prev is None:
                w = (now[1], -now[0]) if sign > 0 else (-now[1], now[0])
            elif sign > 0:
                w = (prev[0] + now[1], prev[1] - now[0])
            else:
                w = (prev[0] - now[1], prev[1] + now[0])
            for b, jj, m in block_pairs(groups):
                if jj == j:
                    add(m, fixed[b], w)
            if j == 3:
                near, far = load(BEYOND), load(BEYOND + 1)
                add(5, near, w)
                add(4, near, now)
                add(5, far, now)
            prev = now
        return acc_re, acc_im

    def body(it, carry):
        row = pl.multiple_of((it % tiles) * rows, rows)
        lane = pl.multiple_of((it // tiles) * lanes, lanes)
        even_re, even_im = products(row, lane, 1)
        for m in range(groups):
            hold[2 * m] = even_re[m]
            hold[2 * m + 1] = even_im[m]
        odd_re, odd_im = products(row + mid, lane, -1)
        for m in range(groups):
            re, im = hold[2 * m], hold[2 * m + 1]
            folded = (re + odd_re[m], im - odd_im[m], re - odd_re[m], im + odd_im[m])
            for part, value in enumerate(folded):
                high, low = split_pair(value)
                at = (pl.ds(row + part * mid, rows), pl.ds(lane, lanes))
                prod[2 * m, at[0], at[1]] = high
                prod[2 * m + 1, at[0], at[1]] = low
        return carry

    def two(it, carry):
        return body(2 * it + 1, body(2 * it, carry))

    lax.fori_loop(0, tiles * (width // lanes) // 2, two, 0)

    rates = rates_ref[:, here]
    tap = lax.broadcasted_iota(jnp.int32, (size, width), 0)
    tap = jnp.where(tap < mid, 2 * tap, 2 * (tap - mid) + 1)
    inner = jnp.exp(-(tap.astype(jnp.float32) / filter_len) * rates)
    head = head_ref[:, here]
    head_high, head_low = split_pair(head)
    for m in range(groups):
        outer = jnp.exp(-(m * size / filter_len) * rates)
        for q in range(2):
            high = prod[2 * m, q * size : (q + 1) * size, :]
            low = prod[2 * m + 1, q * size : (q + 1) * size, :]
            both = dot16(inv_ref[q], high)
            grad = both[:mid] + both[mid:] + dot16(inv_ref[q, :mid, :], low)
            high, low = split_pair(grad * (inner[q * mid : (q + 1) * mid] * outer))
            at = m * size + q * mid
            delta[0, at : at + mid, :] = high
            delta[1, at : at + mid, :] = low
    stacked = dot16(act_ref[...], delta[0])
    total = (
        stacked[: 2 * hidden] + stacked[2 * hidden :] + dot16(act_ref[: 2 * hidden, :], delta[1])
    )
    stacked = dot16(jnp.concatenate([head_high, head_low], axis=0), delta[0], NT)
    second = stacked[:hidden] + stacked[hidden:] + dot16(head_high, delta[1], NT)
    second_ref[...] = second if first else second + second_in[...]

    part_ref[:hidden, :] = total[:hidden]
    part_ref[hidden:, :] = jnp.broadcast_to(
        -jnp.sum(total[hidden:] * head, axis=0, keepdims=True),
        (part_ref.shape[0] - hidden, width),
    )

    if last:
        mix, cols, feats, pre1, act1, cos1, pre2, cos2 = (r[...] for r in net_in)
        mix_freq, emb_freq = cols[:, 3:4], cols[:, 1:2]
        slope2 = second_ref[...] * cos2
        delta2 = slope2 * mix_freq
        slope1 = dot32(mix, delta2) * cos1
        delta1 = slope1 * emb_freq
        count = feats.shape[0]
        net_ref[:, :hidden] = dot32(delta2, act1, NT)
        net_ref[:, hidden : hidden + count] = dot32(delta1, feats, NT)
        for i, value in enumerate((delta1, slope1 * pre1, delta2, slope2 * pre2)):
            at = hidden + count + i
            net_ref[:, at : at + 1] = jnp.sum(value, axis=1, keepdims=True)
        at = hidden + count + 4
        net_ref[:, at:] = jnp.zeros((hidden, net_ref.shape[1] - at), jnp.float32)


def finish_kernel(count, net_ref, far_ref, *rest):
    ew_ref, eb_ref, ef_ref, mw_ref, mb_ref, mf_ref, head_ref, rates_ref = rest[-8:]
    parts = rest[:-8]
    par = lax.axis_index("seq") % 2
    turned = (net_ref[...] + far_ref[...]).T
    hidden = turned.shape[1]
    mw_ref[...] = turned[:hidden]
    ew_ref[...] = turned[hidden : hidden + count]
    for i, ref in enumerate((eb_ref, ef_ref, mb_ref, mf_ref)):
        ref[...] = turned[hidden + count + i : hidden + count + i + 1]
    width = parts[0].shape[1]
    half = head_ref.shape[1] // 2
    for i in range(len(parts) // 2):
        for which, ref in ((par, parts[2 * i]), (1 - par, parts[2 * i + 1])):
            at = pl.ds(pl.multiple_of(which * half + i * width, width), width)
            head_ref[:, at] = ref[:hidden, :]
            rates_ref[:, at] = ref[hidden : hidden + 1, :]


def after(value, *others):
    return lax.optimization_barrier((value, *others))[0]


def work(
    inputs,
    out_grad,
    embed_weight,
    embed_bias,
    embed_freq,
    mixer_weight,
    mixer_bias,
    mixer_freq,
    head_weight,
    decay_rates,
):
    block_len, chan_count = inputs.shape
    hidden = head_weight.shape[0]
    half = chan_count // 2
    size = block_len // 2
    filter_len = SPAN_PARTS * block_len
    groups = filter_len // size
    par = lax.axis_index("seq") % 2
    count = lax.axis_size("seq")
    width = min(256, half)
    chunks = range(half // width)

    def columns(value, which, chunk):
        start = which * half + chunk * width
        return value[:, start : start + width]

    def gives(x_all, g_all, chunk):
        one = jnp.where(par == 0, columns(g_all, 1, chunk), columns(x_all, 0, chunk))
        two = jnp.where(par == 0, columns(x_all, 1, chunk), columns(g_all, 0, chunk))
        return one, two

    odd = (lax.axis_index("seq") // 2) % 2
    ahead = [(i, i + 2) for i in range(0, count - 2, 2)]
    back = [(i, i - 2) for i in range(3, count, 2)]
    upper = [i for i in range(count - 2) if (i // 2) % 2 == 1]
    middle = [(i, i + 2) for i in upper] + [(i + 2, i) for i in upper]

    def halos(x_all, g_all, chunk):
        x_keep = jnp.where(par == 0, columns(x_all, 0, chunk), columns(x_all, 1, chunk))
        g_keep = jnp.where(par == 0, columns(g_all, 0, chunk), columns(g_all, 1, chunk))
        return jnp.where(odd == 0, x_keep, g_keep), jnp.where(odd == 0, g_keep, x_keep)

    e1, e2, s3, za, zb = [], [], [], [], []
    own_in, own_grad = inputs, out_grad
    for c in chunks:
        one, _ = gives(own_in, own_grad, c)
        e1.append(swapped(one, "seq", 1))
        own_in, own_grad, _ = lax.optimization_barrier((own_in, own_grad, one))
    for c in chunks:
        up, down = halos(own_in, own_grad, c)
        za.append(swapped(up, "seq", 2))
        zb.append(lax.ppermute(down, "seq", middle))
        own_in, own_grad, _, _ = lax.optimization_barrier((own_in, own_grad, up, down))
    for c in chunks:
        _, two = gives(own_in, own_grad, c)
        s3.append(lax.ppermute(e1[c], "seq", ahead + back))
        e2.append(swapped(after(two, e1[c]), "seq", 1))

    features = jnp.asarray(tap_features(filter_len, size, BANDS))
    feats = features.shape[0]
    taps = jax.ShapeDtypeStruct((hidden, filter_len), jnp.float32)
    wide = jax.ShapeDtypeStruct((4 * hidden, filter_len), jnp.bfloat16)
    vmem = pl.BlockSpec(memory_space=pltpu.VMEM)
    made = pl.pallas_call(
        prep_kernel,
        in_specs=[vmem] * 7,
        out_specs=[vmem] * 7,
        out_shape=[wide] + [taps] * 5 + [jax.ShapeDtypeStruct((hidden, 8), jnp.float32)],
        compiler_params=pltpu.CompilerParams(vmem_limit_bytes=16 * 2**20),
        name="prep",
    )(
        after(embed_weight, e1[0]),
        embed_bias[None, :],
        embed_freq[None, :],
        mixer_weight,
        mixer_bias[None, :],
        mixer_freq[None, :],
        features,
    )
    act, first_pre, first_act, first_cos, second_pre, second_cos, cols = made

    (fwd_high, fwd_low), (inv_high, inv_low) = transforms(size)
    forward = np.concatenate([fwd_high, fwd_low], axis=0)
    mirrored = forward * np.where(np.arange(4 * size) // size % 2, -1, 1)[:, None].astype(forward.dtype)
    forward = jnp.asarray(np.stack([forward, mirrored]))
    mid = size // 2
    inverse = jnp.asarray(
        np.stack(
            [
                np.concatenate([inv_high[q * mid : (q + 1) * mid], inv_low[q * mid : (q + 1) * mid]])
                for q in range(2)
            ]
        )
    )

    parts = []
    second_grad = None
    late_in, late_grad, _ = lax.optimization_barrier((inputs, out_grad, e1[0]))
    for c in chunks:
        first, last = c == 0, c == chunks[-1]
        operands = [
            late_in,
            late_grad,
            e1[c],
            e2[c],
            za[c],
            zb[c],
            s3[c],
            forward,
            inverse,
            act,
            head_weight,
            decay_rates[None, :],
        ]
        if not first:
            operands.append(second_grad)
        part_shape = jax.ShapeDtypeStruct((hidden + 8, width), jnp.float32)
        second_shape = jax.ShapeDtypeStruct((hidden, filter_len), jnp.float32)
        scratch = [
            pltpu.VMEM((2, block_len, width), jnp.bfloat16),
            pltpu.SemaphoreType.DMA((2,)),
            pltpu.VMEM((14, 2 * size, width), jnp.float32),
            pltpu.VMEM((2 * groups, 2 * size, width), jnp.bfloat16),
            pltpu.VMEM((2 * groups, 16, 128), jnp.float32),
            pltpu.VMEM((2, filter_len, width), jnp.bfloat16),
        ]
        if last:
            operands += [
                mixer_weight,
                cols,
                features,
                first_pre,
                first_act,
                first_cos,
                second_pre,
                second_cos,
            ]
            out_shape = [part_shape, jax.ShapeDtypeStruct((hidden, 2 * hidden), jnp.float32)]
            scratch.append(pltpu.VMEM((hidden, filter_len), jnp.float32))
        else:
            out_shape = [part_shape, second_shape]
        part, out = pl.pallas_call(
            functools.partial(main_kernel, size, groups, filter_len, first, last, c),
            in_specs=[pl.BlockSpec(memory_space=pltpu.HBM)] * 2
            + [pl.BlockSpec(memory_space=pltpu.VMEM)] * (len(operands) - 2),
            out_specs=[pl.BlockSpec(memory_space=pltpu.VMEM)] * 2,
            out_shape=out_shape,
            scratch_shapes=scratch,
            compiler_params=pltpu.CompilerParams(vmem_limit_bytes=40 * 2**20),
            cost_estimate=pl.CostEstimate(
                flops=4 * 10**9, bytes_accessed=8 * 2**20, transcendentals=0
            ),
            name="filter_grad",
        )(*operands)
        parts.append(part)
        if last:
            net = out
        else:
            second_grad = out

    far_bits = bits_of("seq", 2)
    steps = [("chan", b) for b in bits_of("chan")] + [("seq", b) for b in bits_of("seq")]
    for i, (axis, bit) in enumerate(steps):
        far = swapped(net, axis, bit)
        net = net + far if i < len(steps) - 1 else net
    both = []
    for p in parts:
        for bit in far_bits:
            p = p + swapped(p, "seq", bit)
        both += [p, swapped(p, "seq", 1)]

    row = jax.ShapeDtypeStruct((1, hidden), jnp.float32)
    outs = pl.pallas_call(
        functools.partial(finish_kernel, feats),
        in_specs=[pl.BlockSpec(memory_space=pltpu.VMEM)] * (2 + len(both)),
        out_specs=[pl.BlockSpec(memory_space=pltpu.VMEM)] * 8,
        out_shape=[
            jax.ShapeDtypeStruct((feats, hidden), jnp.float32),
            row,
            row,
            jax.ShapeDtypeStruct((hidden, hidden), jnp.float32),
            row,
            row,
            jax.ShapeDtypeStruct((hidden, chan_count), jnp.float32),
            jax.ShapeDtypeStruct((1, chan_count), jnp.float32),
        ],
        compiler_params=pltpu.CompilerParams(vmem_limit_bytes=8 * 2**20),
        name="finish",
    )(net, far, *both)
    return tuple(o[0] if o.shape[0] == 1 else o for o in outs)


def solution(mesh):
    in_specs = (
        P("seq", "chan"),
        P("seq", "chan"),
        P(),
        P(),
        P(),
        P(),
        P(),
        P(),
        P(None, "chan"),
        P("chan"),
    )
    out_specs = (P(), P(), P(), P(), P(), P(), P(None, "chan"), P("chan"))
    return jax.shard_map(work, mesh=mesh, in_specs=in_specs, out_specs=out_specs, check_vma=False)
```
